256 devices in a mesh: leaf: 8 (over x, core), rows: 32 (over z, y).
Axes of the slice: x: 4, y: 4, z: 8, core: 2. Of those that a mesh axis runs over, the one named last changes fastest.
Arguments:
- leaf_inverse: bfloat16 [16384, 2048], P(('leaf', 'rows')), may hold values from -0.125 to 0.125
- leaf_panel: bfloat16 [245760, 2048], P(('leaf', 'rows')), may hold values from -0.0625 to 0.0625
- mid_inverse: bfloat16 [8192, 2048], P(('leaf', 'rows')), may hold values from -0.125 to 0.125
- mid_panel: bfloat16 [122880, 2048], P(('leaf', 'rows')), may hold values from -0.0625 to 0.0625
- top_inverse: bfloat16 [4096, 2048], P(('leaf', 'rows')), may hold values from -0.125 to 0.125
- top_panel: bfloat16 [61440, 2048], P(('leaf', 'rows')), may hold values from -0.0625 to 0.0625
- leaf_rhs: bfloat16 [128, 16384], P(None, ('leaf', 'rows')), may hold values from -6 to 6
- mid_rhs: bfloat16 [128, 8192], P(None, ('leaf', 'rows')), may hold values from -6 to 6
- top_rhs: bfloat16 [128, 4096], P(None, ('leaf', 'rows')), may hold values from -6 to 6
- outer_solution: bfloat16 [128, 61440], P(None, ('leaf', 'rows')), may hold values from -6 to 6
- leaf_targets: int32 [8, 240], replicated, may hold values from -1 to 255, as said below
- mid_targets: int32 [4, 240], replicated, may hold values from -1 to 255, as said below
- front_counts: int32 [14, 2], replicated, may hold values from 128 to 30720, as said below
Outputs:
- leaf_solution: bfloat16 [128, 16384], P(None, ('leaf', 'rows'))
- mid_solution: bfloat16 [128, 8192], P(None, ('leaf', 'rows'))
- top_solution: bfloat16 [128, 4096], P(None, ('leaf', 'rows'))
- top_contribution: bfloat16 [128, 61440], P(None, ('leaf', 'rows'))
The draws below stay inside these ranges and needn't reach their ends.
Inputs may be any that keep to these rules, and one draw needn't show every extreme that they name: `front_counts`: row f gives a front's live pivot count and live update row count, leaf fronts first, then middle, then top fronts. Both are positive multiples of 128, at most 2048 and 30720; top front 0 has 2048 pivots and 30720 update rows. A child's update blocks never outnumber its parent's live blocks. `leaf_targets`: row c lists, for each update block j of leaf front c below its live update rows / 128, the block of middle front c // 2 that receives it, and -1 for the other j. The listed blocks are strictly increasing and live in the parent: below its pivot count / 128, or from 16 up to that plus its update rows / 128. `mid_targets`: row c lists, for each update block j of middle front c below its live update rows / 128, the block of top front c // 2 that receives it, and -1 for the other j. The listed blocks are strictly increasing and live in the parent, as for leaf_targets.
All inputs are finite; a program needn't handle non-finite values.
Results may differ from the reference program's by a relative error of at most 0.019.
Values may be sent and summed in bfloat16 or wider, within the bound.
A program may use at most 64 MiB of HBM per device.

```python
import jax
import jax.numpy as jnp

FRONT_ROWS = 32768
PIVOTS = 2048
UPDATES = 30720
COLUMNS = 128
LEAF_FRONTS = 8
MID_FRONTS = 4
TOP_FRONTS = 2


def choose_blocks(key, wanted, parent_pivots, parent_updates):
    front_blocks = FRONT_ROWS // 128
    pivot_blocks = PIVOTS // 128
    update_blocks = UPDATES // 128
    positions = jnp.arange(front_blocks, dtype=jnp.int32)
    valid = (positions < parent_pivots) | (positions >= pivot_blocks) & (positions < pivot_blocks + parent_updates)
    scores = jax.random.permutation(key, front_blocks).astype(jnp.int32)
    scores = jnp.where(valid, scores, scores + front_blocks)
    order = jnp.argsort(scores, stable=True)
    ranks = jnp.zeros(front_blocks, jnp.int32).at[order].set(positions)
    chosen = valid & (ranks < wanted)
    listed = jnp.sort(jnp.where(chosen, positions, front_blocks))[:update_blocks]
    return jnp.where(listed < front_blocks, listed, -1).astype(jnp.int32)


def tree_layout(key):
    pivot_blocks = PIVOTS // 128
    update_blocks = UPDATES // 128
    low_pivots = max(pivot_blocks // 2, 1)
    low_updates = max(update_blocks // 2, 1)
    seeds = jax.random.split(jax.random.fold_in(key, 7311), 8)
    top_piv = jax.random.randint(seeds[0], (TOP_FRONTS,), low_pivots, pivot_blocks + 1).astype(jnp.int32)
    top_upd = jax.random.randint(seeds[1], (TOP_FRONTS,), low_updates, update_blocks + 1).astype(jnp.int32)
    top_piv = top_piv.at[0].set(pivot_blocks)
    top_upd = top_upd.at[0].set(update_blocks)
    mid_parent = jnp.arange(MID_FRONTS) // 2
    mid_piv = jax.random.randint(seeds[2], (MID_FRONTS,), low_pivots, pivot_blocks + 1).astype(jnp.int32)
    mid_upd = jax.random.randint(seeds[3], (MID_FRONTS,), low_updates, update_blocks + 1).astype(jnp.int32)
    mid_upd = jnp.minimum(mid_upd, top_piv[mid_parent] + top_upd[mid_parent])
    leaf_parent = jnp.arange(LEAF_FRONTS) // 2
    leaf_piv = jax.random.randint(seeds[4], (LEAF_FRONTS,), low_pivots, pivot_blocks + 1).astype(jnp.int32)
    leaf_upd = jax.random.randint(seeds[5], (LEAF_FRONTS,), low_updates, update_blocks + 1).astype(jnp.int32)
    leaf_upd = jnp.minimum(leaf_upd, mid_piv[leaf_parent] + mid_upd[leaf_parent])
    pivots_all = jnp.concatenate([leaf_piv, mid_piv, top_piv]) * 128
    updates_all = jnp.concatenate([leaf_upd, mid_upd, top_upd]) * 128
    counts_table = jnp.stack([pivots_all, updates_all], axis=1).astype(jnp.int32)
    leaf_list = jax.vmap(choose_blocks)(jax.random.split(seeds[6], LEAF_FRONTS), leaf_upd, mid_piv[leaf_parent], mid_upd[leaf_parent])
    mid_list = jax.vmap(choose_blocks)(jax.random.split(seeds[7], MID_FRONTS), mid_upd, top_piv[mid_parent], top_upd[mid_parent])
    return (counts_table, leaf_list, mid_list)


def draw_front_counts(key, part):
    return tree_layout(key)[0]


def draw_leaf_targets(key, part):
    return tree_layout(key)[1]


def draw_mid_targets(key, part):
    return tree_layout(key)[2]


def level_of(key, shape, shards, low, largest):
    level, own = 1.0, jax.random.fold_in(key, 6)
    for dim, parts in shards:
        steps = jnp.exp(jax.random.uniform(jax.random.fold_in(own, dim), (parts,), jnp.float32, low / len(shards), largest / len(shards)))
        level = level * jnp.repeat(steps, shape[dim] // parts).reshape([-1 if axis == dim else 1 for axis in range(len(shape))])
    return level


def noise(own_key, extent, deviation, reach, cuts=(), kind=jnp.bfloat16):
    factor_of = level_of(own_key, extent, cuts, -0.22, 0.18) if cuts else 1.0
    result = jax.random.normal(own_key, extent, jnp.float32) * deviation * factor_of
    return jnp.minimum(jnp.maximum(result, -reach), reach).astype(kind)


def setup_inputs(seed: int = 0) -> dict:
    splits = jax.random.split(jax.random.key(seed), 14)
    return {
        "leaf_inverse": noise(splits[0], (LEAF_FRONTS * PIVOTS, PIVOTS), PIVOTS ** -0.5, 0.125, ((0, 256),)),
        "leaf_panel": noise(splits[1], (LEAF_FRONTS * UPDATES, PIVOTS), (4 * PIVOTS) ** -0.5, 0.0625, ((0, 256),)),
        "mid_inverse": noise(splits[2], (MID_FRONTS * PIVOTS, PIVOTS), PIVOTS ** -0.5, 0.125, ((0, 256),)),
        "mid_panel": noise(splits[3], (MID_FRONTS * UPDATES, PIVOTS), (4 * PIVOTS) ** -0.5, 0.0625, ((0, 256),)),
        "top_inverse": noise(splits[4], (TOP_FRONTS * PIVOTS, PIVOTS), PIVOTS ** -0.5, 0.125, ((0, 256),)),
        "top_panel": noise(splits[5], (TOP_FRONTS * UPDATES, PIVOTS), (4 * PIVOTS) ** -0.5, 0.0625, ((0, 256),)),
        "leaf_rhs": noise(splits[6], (COLUMNS, LEAF_FRONTS * PIVOTS), 1.0, 6.0, ((1, 256),)),
        "mid_rhs": noise(splits[7], (COLUMNS, MID_FRONTS * PIVOTS), 1.0, 6.0, ((1, 256),)),
        "top_rhs": noise(splits[8], (COLUMNS, TOP_FRONTS * PIVOTS), 1.0, 6.0, ((1, 256),)),
        "outer_solution": noise(splits[9], (COLUMNS, TOP_FRONTS * UPDATES), 1.0, 6.0, ((1, 256),)),
        "leaf_targets": draw_leaf_targets(jax.random.fold_in(splits[13], 71), 0),
        "mid_targets": draw_mid_targets(jax.random.fold_in(splits[13], 71), 0),
        "front_counts": draw_front_counts(jax.random.fold_in(splits[13], 71), 0),
    }


def live_columns(length, count):
    return (jnp.arange(length) < count)[None, :]


def spread_blocks(update, targets):
    blocks = FRONT_ROWS // 128
    pieces = update.astype(jnp.float32).reshape(update.shape[0], -1, 128)
    placed = jnp.where(targets >= 0, targets, blocks).astype(jnp.int32)
    buffer = jnp.zeros((update.shape[0], blocks + 1, 128), jnp.float32)
    buffer = buffer.at[:, placed].add(pieces)
    return buffer[:, :blocks].reshape(update.shape[0], FRONT_ROWS)


def pick_blocks(parent_full, targets):
    blocks = FRONT_ROWS // 128
    pieces = parent_full.reshape(parent_full.shape[0], blocks, 128)
    picked = pieces[:, jnp.maximum(targets, 0).astype(jnp.int32)]
    picked = jnp.where((targets >= 0)[None, :, None], picked, jnp.zeros_like(picked))
    return picked.reshape(parent_full.shape[0], -1)


def reference(leaf_inverse, leaf_panel, mid_inverse, mid_panel, top_inverse, top_panel,
              leaf_rhs, mid_rhs, top_rhs, outer_solution, leaf_targets, mid_targets, front_counts):
    inverses = (leaf_inverse, mid_inverse, top_inverse)
    panels = (leaf_panel, mid_panel, top_panel)
    sources = (leaf_rhs, mid_rhs, top_rhs)
    targets = (leaf_targets, mid_targets)
    offsets = (0, LEAF_FRONTS, LEAF_FRONTS + MID_FRONTS)
    numbers = (LEAF_FRONTS, MID_FRONTS, TOP_FRONTS)
    forward = []
    spreads = []
    for height in range(3):
        results = []
        new_spreads = []
        for front_index in range(numbers[height]):
            pivot_count = front_counts[offsets[height] + front_index, 0]
            update_count = front_counts[offsets[height] + front_index, 1]
            inverse = inverses[height][front_index * PIVOTS:(front_index + 1) * PIVOTS]
            panel_rows = panels[height][front_index * UPDATES:(front_index + 1) * UPDATES]
            if height == 0:
                gathered = jnp.zeros((COLUMNS, FRONT_ROWS), jnp.float32)
            else:
                gathered = spreads[2 * front_index] + spreads[2 * front_index + 1]
            source = sources[height][:, front_index * PIVOTS:(front_index + 1) * PIVOTS].astype(jnp.float32)
            assembled = source + gathered[:, :PIVOTS]
            assembled = jnp.where(live_columns(PIVOTS, pivot_count), assembled, jnp.zeros_like(assembled)).astype(jnp.bfloat16)
            solved = jnp.dot(assembled, inverse.T, preferred_element_type=jnp.float32)
            solved = jnp.where(live_columns(PIVOTS, pivot_count), solved, jnp.zeros_like(solved)).astype(jnp.bfloat16)
            update = gathered[:, PIVOTS:] - jnp.dot(assembled, panel_rows.T, preferred_element_type=jnp.float32)
            update = jnp.where(live_columns(UPDATES, update_count), update, jnp.zeros_like(update)).astype(jnp.bfloat16)
            results.append((solved, update))
            if height < 2:
                new_spreads.append(spread_blocks(update, targets[height][front_index]))
        forward.append(results)
        spreads = new_spreads
    solutions = [None, None, None]
    fulls = []
    for height in (2, 1, 0):
        pieces = []
        new_fulls = []
        for front_index in range(numbers[height]):
            pivot_count = front_counts[offsets[height] + front_index, 0]
            update_count = front_counts[offsets[height] + front_index, 1]
            inverse = inverses[height][front_index * PIVOTS:(front_index + 1) * PIVOTS]
            panel_rows = panels[height][front_index * UPDATES:(front_index + 1) * UPDATES]
            if height == 2:
                given_rows = outer_solution[:, front_index * UPDATES:(front_index + 1) * UPDATES]
            else:
                given_rows = pick_blocks(fulls[front_index // 2], targets[height][front_index])
            given_rows = jnp.where(live_columns(UPDATES, update_count), given_rows, jnp.zeros_like(given_rows))
            solved = forward[height][front_index][0]
            solution = jnp.dot(solved, inverse, preferred_element_type=jnp.float32) - jnp.dot(given_rows, panel_rows, preferred_element_type=jnp.float32)
            solution = jnp.where(live_columns(PIVOTS, pivot_count), solution, jnp.zeros_like(solution)).astype(jnp.bfloat16)
            pieces.append(solution)
            new_fulls.append(jnp.concatenate([solution, given_rows], axis=1))
        solutions[height] = jnp.concatenate(pieces, axis=1)
        fulls = new_fulls
    top_contribution = jnp.concatenate([entry[1] for entry in forward[2]], axis=1)
    return solutions[0], solutions[1], solutions[2], top_contribution
```

```python
import jax
import jax.numpy as jnp
from jax import lax
from jax.experimental import pallas as pl
from jax.experimental.pallas import tpu as pltpu
from jax.sharding import PartitionSpec as P

MESH = pl.DeviceIdType.MESH
BF = jnp.bfloat16
F32 = jnp.float32
R = 32

(EA, A1, X1, D1, A2, RT, ZG, P3, U3, D2, CR, HX2, XX2, ZX2, GR1, ZGM, OT, HX1, ZX1, OM, GR0,
 AG0, G1, G2, RS2, RS1, RS0) = tuple(range(21)) + tuple(range(21, 21 + 54, 9))
NSEM = 21 + 54


def pieces(rows, period):
    out = {}
    for d in range(period):
        start = rows * d
        first = start // 128
        last = (start + rows - 1) // 128
        for b in range(first, last + 1):
            out.setdefault(b, []).append((d, b - first))
    return [out[b] for b in range(rows * period // 128)]


MID_PIECES = pieces(480, 4)
TOP_PIECES = pieces(240, 8)


def kernel(
    rhs0, rhs1, rhs2, outer, w0, q0, w1, q1, w2, q2, ltv, mtv, lt, mt, cnt,
    o_leaf, o_mid, o_top, o_con,
    wp0, wp1, wp2, qv0, qv1, qv2, at0, e, at, a, y0, y1, y2, le, sb1, lb1, sp1, rp1, c1, rm, sba1, la1, sb2, lb2, vm,
    s3p, r3p, s3u, r3u, rtq, sba2, la2, gtq, zt, ct, lc, g2, xpt, sbx, rbx, sby, ry, sz, lz, xs2, xx2, gm, zm, lg1,
    g1, sbx1, rbx1, sby1, ry1, sz1, lz1, xsb1, gl, lg0, g0, sbl, ryl, szl, lzl, lot, lom,
    tmp, invv, inv, isem, wsem, ssem, rsem,
):
    s = lax.axis_index("leaf")
    r = lax.axis_index("rows")
    c = s % 2
    w4 = s % 4
    z = r // 4
    y = r % 4
    xb = (s // 2) % 2
    m1 = c * R + r
    m2 = w4 * R + r
    p1 = s + 1 - 2 * c
    p2 = s + 2 - 4 * xb
    p3 = p2 + 1 - 2 * c
    partners = (p1, p2, p3)

    barrier = pltpu.get_barrier_semaphore()

    def greet(k, _):
        pl.semaphore_signal(barrier, inc=1, device_id=(s, (r + k) % R), device_id_type=MESH)
        return 0

    lax.fori_loop(1, R, greet, 0)
    for p in partners:
        pl.semaphore_signal(barrier, inc=1, device_id=(p, r), device_id_type=MESH)

    off0 = pl.multiple_of((r % 2) * 64, 64)
    off1 = pl.multiple_of((r % 4) * 96 % 128, 32)
    off2 = pl.multiple_of((r % 8) * 112 % 128, 16)
    loads = []
    for k, (src, dst) in enumerate((
        (w0, wp0.at[pl.ds(off0, 960)]), (q0, qv0), (w1, wp1.at[pl.ds(off1, 480)]), (q1, qv1),
        (w2, wp2.at[pl.ds(off2, 240)]), (q2, qv2),
    )):
        copy = pltpu.make_async_copy(src, dst, wsem.at[k])
        copy.start()
        loads.append(copy)
    for wp, off, rows in ((wp0, off0, 960), (wp1, off1, 480), (wp2, off2, 240)):
        def zero_pad(t, _, wp=wp, off=off, rows=rows):
            at_row = jnp.where(16 * t < off, 16 * t, 16 * t + rows)
            wp[pl.ds(pl.multiple_of(at_row, 16), 16), :] = jnp.zeros((16, 2048), BF)
            return 0
        lax.fori_loop(0, (wp.shape[0] - rows) // 16, zero_pad, 0)
    zero_block = jnp.zeros((4, 128), BF)
    lb1[0] = zero_block
    vm[0] = zero_block
    vm[121] = zero_block
    ct[60] = zero_block
    zt[0] = zero_block
    zm[0] = zero_block
    gm[120] = zero_block

    piv0, piv1, piv2, upd2 = cnt[0, s], cnt[0, 8 + s // 2], cnt[0, 12 + s // 4], cnt[1, 12 + s // 4]

    def live(pivots, block):
        return jnp.clip(pivots - block * 128, 0, 1).astype(F32)

    f0, f1, f2 = live(piv0, r // 2), live(piv1, m1 // 4), live(piv2, m2 // 8)
    at0[...] = (rhs0[...].astype(F32) * f0).astype(BF)

    place = lax.broadcasted_iota(jnp.int32, (128, 128), 0)
    wanted = lax.broadcasted_iota(jnp.int32, (128, 128), 1)
    for row, (values, here) in enumerate(((ltv, s), (mtv, s // 2))):
        line = values[pl.ds(here, 1), :]
        parts = [line[:, :128], jnp.concatenate([line[:, 128:], jnp.full((1, 16), -1, jnp.int32)], axis=1)]
        found = [jnp.zeros((1, 128), jnp.int32)] * 2
        for k in range(2):
            target = jnp.broadcast_to(parts[k], (128, 128)).T
            j = place + 128 * k
            if row == 0:
                j = 1 + j + j // 15 + (j % 15 > 7).astype(jnp.int32)
            else:
                j = 1 + j
            for h in range(2):
                hit = jnp.where(target == wanted + 128 * h, j, 0)
                found[h] = found[h] + jnp.sum(hit, axis=0, keepdims=True)
        for h in range(2):
            invv[2 * row + h:2 * row + h + 1, :] = found[h]
    table = pltpu.make_async_copy(invv, inv, isem)
    table.start()

    def block_rows(x, rows, first):
        tmp[0:rows] = jnp.zeros((rows, 128), F32)
        tmp[pl.ds(pl.multiple_of(first, 16), x.shape[0]), :] = x
        return [tmp[b * 128:(b + 1) * 128].T for b in range(rows // 128)]

    e[:, 0] = block_rows(rhs1[...].astype(F32) * f1, 128, 32 * (r % 4))[0].reshape(R, 4, 128).astype(BF)
    e[:, 1] = block_rows(rhs2[...].astype(F32) * f2, 128, 16 * (r % 8))[0].reshape(R, 4, 128).astype(BF)
    row240 = lax.broadcasted_iota(jnp.int32, (240, 128), 0)
    given = jnp.where(row240 < upd2 - 240 * m2, outer[...].astype(F32), 0.0)
    for b, v in enumerate(block_rows(given, 384, off2)):
        g2[:, b * 128:(b + 1) * 128] = v.astype(BF)
        e[:, 2 + b] = v.reshape(R, 4, 128).astype(BF)

    pl.semaphore_wait(barrier, R - 1 + 3)

    landed = {}

    def remote(src, dst, n, dev, land):
        landed[n] = [land, False]
        return pltpu.make_async_remote_copy(
            src_ref=src, dst_ref=dst, send_sem=ssem.at[n], recv_sem=rsem.at[n], device_id=dev, device_id_type=MESH
        )

    def to_rows(src_of, dst, n, land):
        def send(k, _):
            d = (r + k) % R
            remote(src_of(d), dst, n, (s, d), land).start()
            return 0

        lax.fori_loop(1, R, send, 0)

    def arrived(n):
        ref = landed[n][0]
        landed[n][1] = True
        pltpu.make_async_copy(ref, ref, rsem.at[n]).wait()

    def sent(n):
        ref = landed[n][0]
        pltpu.make_async_copy(ref, ref, ssem.at[n]).wait()

    def gather(mine, dst, n, piece):
        def along_y(src, k):
            for j in (1, 3, 2):
                remote(src, dst(k), n, (s, z * 4 + (y + j) % 4), piece(24)).start()

        for k in (4, 3, 5, 2, 6, 1, 7):
            remote(mine, dst(r), n + k, (s, (z + k) % 8 * 4 + y), piece(1)).start()
        along_y(mine, r)
        for k in (1, 7, 2, 6, 3, 5, 4):
            arrived(n + k)
            other = (z + 8 - k) % 8 * 4 + y
            along_y(dst(other), other)
        arrived(n)

    def reduce_y(src, land, n, o, piece):
        t = (z + o) % 8
        for j in (1, 3, 2):
            remote(src(4 * t + (y + j) % 4), land.at[o, j - 1], n + o, (s, z * 4 + (y + j) % 4), piece(3)).start()

    def reduce_z(src, land, stage, final, n, o, piece):
        t = (z + o) % 8
        arrived(n + o)
        v = src[4 * t + y].astype(F32) + land[o, 0].astype(F32) + land[o, 1].astype(F32) + land[o, 2].astype(F32)
        if o == 0:
            return v
        stage[o - 1] = v.astype(BF)
        remote(stage.at[o - 1], final.at[o - 1], n + 8, (s, t * 4 + y), piece(7)).start()

    ORDER = (1, 2, 3, 4, 5, 6, 7, 0)

    def nt(x, w):
        return lax.dot_general(x, w, (((1,), (1,)), ((), ())), preferred_element_type=F32)

    at[r] = at0[...]
    gather(at0, lambda k: at.at[k], AG0, lambda k: at.at[pl.ds(0, k)])
    to_rows(lambda d: e.at[d], le.at[r], EA, le.at[pl.ds(0, R - 1)])
    le[r] = e[r]
    for k in range(16):
        block = at[2 * k:2 * k + 2].reshape(128, 128)
        a[:, k * 128:(k + 1) * 128] = block.T
    loads[0].wait()
    loads[1].wait()

    def leaf_update(t, _):
        prod = -nt(a[...], wp0[pl.ds(pl.multiple_of(t * 256, 256), 256), :])
        for b in range(2):
            sb1[:, 2 * t + b] = prod[:, b * 128:(b + 1) * 128].reshape(R, 4, 128).astype(BF)
        return 0

    lax.fori_loop(0, 4, leaf_update, 0)
    to_rows(lambda d: sb1.at[d], lb1.at[pl.ds(1 + r * 8, 8)], A1, lb1.at[pl.ds(0, 8 * (R - 1))])
    lb1[pl.ds(1 + r * 8, 8)] = sb1[r]
    y0[...] = (nt(a[...], qv0[...]) * f0).astype(BF)

    arrived(EA)
    for b in range(8):
        rm[b] = sum(le[4 * b + i, 0].astype(F32) for i in range(4))
    for b in range(4):
        rtq[4 * w4 + b] = sum(le[8 * b + i, 1].astype(F32) for i in range(8)).astype(BF)

    def outer_merge(q, _):
        for i, parts in enumerate(TOP_PIECES):
            v = sum(le[8 * q + d, 2 + k].astype(F32) for d, k in parts).astype(BF)
            gtq[15 * q + i] = v
            zt[17 + 60 * w4 + 15 * q + i] = v
        return 0

    lax.fori_loop(0, 4, outer_merge, 0)
    for p in partners:
        remote(rtq.at[pl.ds(4 * w4, 4)], rtq.at[pl.ds(4 * w4, 4)], RT, (p, r), rtq.at[pl.ds(0, 12)]).start()
        remote(gtq, zt.at[pl.ds(17 + 60 * w4, 60)], ZG, (p, r), zt.at[pl.ds(16, 180)]).start()
    loads[4].wait()
    loads[5].wait()

    def top_given(t, _):
        cols = pl.ds(pl.multiple_of(t * 256, 256), 256)
        xpt[:, cols] = -jnp.dot(g2[...], wp2[:, cols], preferred_element_type=F32)
        return 0

    lax.fori_loop(0, 8, top_given, 0)

    arrived(A1)
    table.wait()

    def leaf_merge(q, _):
        lb1[16 * q + 8] = (lb1[16 * q + 8].astype(F32) + lb1[16 * q + 9].astype(F32)).astype(BF)
        return 0

    lax.fori_loop(0, 16, leaf_merge, 0)

    def child_block(core, j):
        b = jnp.where(j < 8, 8 * core, 8 + 120 * core) + j
        return jnp.clip(inv[b // 128, b % 128], 0, 256)

    def for_partner(j, _):
        sp1[j] = lb1[child_block(1 - c, j)]
        return 0

    lax.fori_loop(0, 128, for_partner, 0, unroll=8)
    remote(sp1, rp1, X1, (p1, r), rp1).start()

    def for_own(j, _):
        c1[j] = lb1[child_block(c, j)].astype(F32)
        return 0

    lax.fori_loop(0, 128, for_own, 0, unroll=8)
    arrived(X1)
    c1[...] = c1[...] + rp1[...].astype(F32)

    sba1[...] = (rm[...] + c1[0:8]).astype(BF)
    la1[c, r] = sba1[...]
    gather(sba1, lambda k: la1.at[c, k], G1, lambda k: la1.at[0, pl.ds(0, k)])
    remote(la1.at[c], la1.at[c], D1, (p1, r), la1.at[1 - c]).start()
    arrived(D1)
    for h in range(2):
        for b in range(8):
            a[:, (8 * h + b) * 128:(8 * h + b + 1) * 128] = la1[h, :, b].reshape(128, 128)
    loads[2].wait()
    loads[3].wait()

    def mid_update(t, _):
        prod = nt(a[...], wp1[pl.ds(pl.multiple_of(t * 128, 128), 128), :])
        sb2[:, t] = prod.reshape(R, 4, 128).astype(BF)
        return 0

    lax.fori_loop(0, 5, mid_update, 0)
    to_rows(lambda d: sb2.at[d], lb2.at[r], A2, lb2.at[pl.ds(0, R - 1)])
    lb2[r] = sb2[r]
    y1[...] = (nt(a[...], qv1[...]) * f1).astype(BF)
    arrived(A2)

    def mid_merge(q, _):
        for i, parts in enumerate(MID_PIECES):
            v = c1[8 + 15 * q + i] - sum(lb2[4 * q + d, k].astype(F32) for d, k in parts)
            vm[1 + 15 * q + i] = v.astype(BF)
        return 0

    lax.fori_loop(0, 8, mid_merge, 0)

    def parent_block(j):
        return jnp.clip(inv[2 + j // 128, j % 128] - 120 * c, 0, 121)

    for j in range(16):
        s3p[j] = vm[parent_block(j)]
    for k, p in enumerate(partners):
        remote(s3p, r3p.at[k], P3, (p, r), r3p).start()
    for k in range(3):
        def top_spread(j, _, k=k):
            s3u[k, j] = vm[parent_block(16 + 60 * (partners[k] % 4) + j)]
            return 0

        lax.fori_loop(0, 60, top_spread, 0, unroll=4)
        remote(s3u.at[k], r3u.at[k], U3, (partners[k], r), r3u).start()
    arrived(RT)
    arrived(P3)
    for j in range(16):
        v = rtq[j].astype(F32) + s3p[j].astype(F32) + sum(r3p[k, j].astype(F32) for k in range(3))
        sba2[j] = v.astype(BF)
    la2[c, r] = sba2[pl.ds(8 * c, 8)]
    gather(sba2.at[pl.ds(8 * c, 8)], lambda k: la2.at[c, k], G2, lambda k: la2.at[0, pl.ds(0, k)])
    arrived(U3)

    def top_sum(j, _):
        v = vm[parent_block(16 + 60 * w4 + j)].astype(F32) + sum(r3u[k, j].astype(F32) for k in range(3))
        ct[j] = v.astype(BF)
        return 0

    lax.fori_loop(0, 60, top_sum, 0, unroll=4)
    remote(la2.at[c], la2.at[c], D2, (p1, r), la2.at[1 - c]).start()
    to_rows(lambda d: ct.at[pl.ds(240 * d // 128, 3)], lc.at[r], CR, lc.at[pl.ds(0, R - 1)])
    lc[r] = ct[pl.ds(240 * r // 128, 3)]
    arrived(D2)
    for h in range(2):
        for b in range(8):
            a[:, (8 * h + b) * 128:(8 * h + b + 1) * 128] = la2[h, :, b].reshape(128, 128)
    y2[...] = (nt(a[...], qv2[...]) * f2).astype(BF)

    def top_partial(t, _):
        cols = pl.ds(pl.multiple_of(t * 256, 256), 256)
        v = xpt[:, cols] + jnp.dot(y2[...], qv2[:, cols], preferred_element_type=F32)
        for b in range(2):
            sbx[t // 4, :, 2 * (t % 4) + b] = v[:, b * 128:(b + 1) * 128].reshape(R, 4, 128).astype(BF)
        return 0

    lax.fori_loop(0, 8, top_partial, 0)
    remote(sbx.at[1 - c], rbx, HX2, (p1, r), rbx).start()
    prod = nt(a[...], wp2[...])
    arrived(CR)
    for b in range(3):
        v = lc[:, b].astype(F32).reshape(128, 128) - prod[:, b * 128:(b + 1) * 128]
        tmp[b * 128:(b + 1) * 128] = v.T
    o_con[...] = jnp.where(row240 < upd2 - 240 * m2, tmp[pl.ds(off2, 240), :], 0.0).astype(BF)
    arrived(HX2)

    def reduce_half(mine, other, both, land, stage, final, n):
        for o in ORDER:
            t = (z + o) % 8
            rows4 = pl.ds(4 * t, 4)
            both[rows4] = (mine[c, rows4].astype(F32) + other[rows4].astype(F32)).astype(BF)
            reduce_y(lambda d: both.at[d], land, n, o, lambda k: land.at[0, pl.ds(0, k)])
        for o in ORDER:
            v = reduce_z(both, land, stage, final, n, o, lambda k: final.at[pl.ds(0, k)])
        arrived(n + 8)
        for o in range(7):
            v = v + final[o].astype(F32)
        return v

    xs2[...] = reduce_half(sbx, rbx, sby, ry, sz, lz, RS2)
    remote(xs2, xx2, XX2, (p2, r), xx2).start()
    arrived(XX2)
    for b in range(8):
        zt[1 + 8 * c + b] = ((xs2[b] + xx2[b]) * live(piv2, 8 * c + b)).astype(BF)
    remote(zt.at[pl.ds(1 + 8 * c, 8)], zt.at[pl.ds(1 + 8 * c, 8)], ZX2, (p1, r), zt.at[pl.ds(0, 8)]).start()
    arrived(ZX2)
    arrived(ZG)

    def mid_pick(j, _):
        v = zt[mt[s // 2, 120 * c + j] + 1]
        gm[j] = v
        zm[17 + 120 * c + j] = v
        return 0

    lax.fori_loop(0, 120, mid_pick, 0, unroll=8)
    to_rows(lambda d: gm.at[pl.ds(480 * d // 128, 5)], lg1.at[r], GR1, lg1.at[pl.ds(0, R - 1)])
    lg1[r] = gm[pl.ds(480 * r // 128, 5)]
    remote(gm.at[pl.ds(0, 120)], zm.at[pl.ds(17 + 120 * c, 120)], ZGM, (p1, r), zm.at[pl.ds(0, 120)]).start()
    to_rows(lambda d: zt.at[1 + 4 * w4 + d // 8], lot.at[r], OT, lot.at[pl.ds(0, R - 1)])
    lot[r] = zt[1 + 4 * w4 + r // 8]
    arrived(GR1)
    for b in range(5):
        g1[:, b * 128:(b + 1) * 128] = lg1[:, b].reshape(128, 128)

    def mid_partial(t, _):
        cols = pl.ds(pl.multiple_of(t * 256, 256), 256)
        v = jnp.dot(y1[...], qv1[:, cols], preferred_element_type=F32) - jnp.dot(
            g1[...], wp1[:, cols], preferred_element_type=F32
        )
        for b in range(2):
            sbx1[t // 4, :, 2 * (t % 4) + b] = v[:, b * 128:(b + 1) * 128].reshape(R, 4, 128).astype(BF)
        return 0

    lax.fori_loop(0, 8, mid_partial, 0)
    remote(sbx1.at[1 - c], rbx1, HX1, (p1, r), rbx1).start()
    arrived(HX1)
    xsum = reduce_half(sbx1, rbx1, sby1, ry1, sz1, lz1, RS1)
    for b in range(8):
        v = (xsum[b] * live(piv1, 8 * c + b)).astype(BF)
        xsb1[b] = v
        zm[1 + 8 * c + b] = v
    remote(xsb1, zm.at[pl.ds(1 + 8 * c, 8)], ZX1, (p1, r), zm.at[pl.ds(0, 8)]).start()
    arrived(ZX1)
    arrived(ZGM)

    def leaf_pick(j, _):
        gl[j] = zm[lt[s, j] + 1]
        return 0

    lax.fori_loop(0, 240, leaf_pick, 0, unroll=8)
    to_rows(lambda d: gl.at[pl.ds(960 * d // 128, 8)], lg0.at[r], GR0, lg0.at[pl.ds(0, R - 1)])
    lg0[r] = gl[pl.ds(960 * r // 128, 8)]
    to_rows(lambda d: xsb1.at[d // 4], lom.at[r], OM, lom.at[pl.ds(0, R - 1)])
    lom[r] = xsb1[r // 4]
    arrived(OT)
    tmp[0:128] = lot[...].astype(F32).reshape(128, 128).T
    o_top[...] = tmp[pl.ds(pl.multiple_of(16 * (r % 8), 16), 16), :].astype(BF)
    arrived(GR0)
    for b in range(8):
        g0[:, b * 128:(b + 1) * 128] = lg0[:, b].reshape(128, 128)

    def leaf_tile(o):
        t = (z + o) % 8
        cols = pl.ds(pl.multiple_of(t * 256, 256), 256)
        v = jnp.dot(y0[...], qv0[:, cols], preferred_element_type=F32) - jnp.dot(
            g0[...], wp0[:, cols], preferred_element_type=F32
        )
        sbl[pl.ds(4 * t, 4)] = v.T.astype(BF).reshape(4, 64, 128)
        reduce_y(lambda d: sbl.at[d], ryl, RS0, o, lambda k: ryl.at[0, pl.ds(0, k)])

    def leaf_sum(o):
        return reduce_z(sbl, ryl, szl, lzl, RS0, o, lambda k: lzl.at[pl.ds(0, k)])

    for k in range(8):
        leaf_tile(ORDER[k])
        if k >= 3:
            leaf_sum(ORDER[k - 3])
    for k in range(5, 8):
        xl = leaf_sum(ORDER[k])
    arrived(OM)
    tmp[0:128] = lom[...].astype(F32).reshape(128, 128).T
    o_mid[...] = tmp[pl.ds(pl.multiple_of(32 * (r % 4), 32), 32), :].astype(BF)
    arrived(RS0 + 8)
    for o in range(7):
        xl = xl + lzl[o].astype(F32)
    o_leaf[...] = (xl * f0).astype(BF)

    for n in landed:
        sent(n)


SCRATCH = [
    ((1024, 2048), BF), ((640, 2048), BF), ((384, 2048), BF), ((64, 2048), BF), ((32, 2048), BF), ((16, 2048), BF),
    ((64, 128), BF), ((R, 5, 4, 128), BF),
    ((R, 64, 128), BF), ((128, 2048), BF), ((128, 64), BF), ((128, 32), BF), ((128, 16), BF), ((R, 5, 4, 128), BF),
    ((R, 8, 4, 128), BF), ((264, 4, 128), BF), ((128, 4, 128), BF), ((128, 4, 128), BF), ((128, 4, 128), F32),
    ((8, 4, 128), F32), ((8, 4, 128), BF), ((2, R, 8, 4, 128), BF), ((R, 5, 4, 128), BF), ((R, 5, 4, 128), BF),
    ((122, 4, 128), BF),
    ((16, 4, 128), BF), ((3, 16, 4, 128), BF), ((3, 60, 4, 128), BF), ((3, 60, 4, 128), BF), ((16, 4, 128), BF),
    ((16, 4, 128), BF), ((2, R, 8, 4, 128), BF), ((60, 4, 128), BF), ((257, 4, 128), BF), ((61, 4, 128), BF),
    ((R, 3, 4, 128), BF), ((128, 384), BF), ((128, 2048), F32), ((2, R, 8, 4, 128), BF), ((R, 8, 4, 128), BF),
    ((R, 8, 4, 128), BF), ((8, 3, 8, 4, 128), BF), ((7, 8, 4, 128), BF), ((7, 8, 4, 128), BF), ((8, 4, 128), F32), ((8, 4, 128), F32), ((121, 4, 128), BF),
    ((257, 4, 128), BF), ((R, 5, 4, 128), BF), ((128, 640), BF),
    ((2, R, 8, 4, 128), BF), ((R, 8, 4, 128), BF), ((R, 8, 4, 128), BF), ((8, 3, 8, 4, 128), BF), ((7, 8, 4, 128), BF), ((7, 8, 4, 128), BF), ((8, 4, 128), BF),
    ((240, 4, 128), BF), ((R, 8, 4, 128), BF), ((128, 1024), BF), ((R, 64, 128), BF), ((8, 3, 64, 128), BF),
    ((7, 64, 128), BF), ((7, 64, 128), BF),
    ((R, 4, 128), BF), ((R, 4, 128), BF),
]


def hand_over(*refs):
    for k in range(4):
        refs[4 + k][...] = refs[k][...]


def body(
    leaf_inverse, leaf_panel, mid_inverse, mid_panel, top_inverse, top_panel,
    leaf_rhs, mid_rhs, top_rhs, outer_solution, leaf_targets, mid_targets, front_counts,
):
    vmem = pl.BlockSpec(memory_space=pltpu.VMEM)
    smem = pl.BlockSpec(memory_space=pltpu.SMEM)
    hbm = pl.BlockSpec(memory_space=pl.ANY)
    outs = pl.pallas_call(
        kernel,
        out_shape=tuple(jax.ShapeDtypeStruct((n, 128), BF) for n in (64, 32, 16, 240)),
        in_specs=[vmem] * 4 + [hbm] * 6 + [vmem] * 2 + [smem] * 3,
        out_specs=(vmem,) * 4,
        scratch_shapes=[pltpu.VMEM(shape, kind) for shape, kind in SCRATCH]
        + [pltpu.VMEM((384, 128), F32), pltpu.VMEM((8, 128), jnp.int32), pltpu.SMEM((8, 128), jnp.int32)]
        + [pltpu.SemaphoreType.DMA, pltpu.SemaphoreType.DMA((6,)), pltpu.SemaphoreType.DMA((NSEM,)), pltpu.SemaphoreType.DMA((NSEM,))],
        compiler_params=pltpu.CompilerParams(
            collective_id=0, has_side_effects=True, vmem_limit_bytes=56 * 1024 * 1024
        ),
        name="solve",
    )(
        leaf_rhs.T, mid_rhs.T, top_rhs.T, outer_solution.T,
        leaf_panel, leaf_inverse, mid_panel, mid_inverse, top_panel, top_inverse,
        leaf_targets, mid_targets, leaf_targets, mid_targets, front_counts.T,
    )
    shapes = tuple(jax.ShapeDtypeStruct(out.shape, BF) for out in outs)
    outs = pl.pallas_call(hand_over, out_shape=shapes, in_specs=[vmem] * 4, out_specs=(vmem,) * 4, name="hand_over")(*outs)
    return tuple(out.T for out in outs)


def solution(mesh):
    stacked = P(("leaf", "rows"), None)
    side = P(None, ("leaf", "rows"))
    return jax.shard_map(
        body,
        mesh=mesh,
        in_specs=(stacked,) * 6 + (side,) * 4 + (P(),) * 3,
        out_specs=(side,) * 4,
        check_vma=False,
    )
```

```python
import jax
import jax.numpy as jnp
from jax import lax
from jax.experimental import pallas as pl
from jax.experimental.pallas import tpu as pltpu
from jax.sharding import PartitionSpec as P

MESH = pl.DeviceIdType.MESH
BF = jnp.bfloat16
F32 = jnp.float32
R = 32

(EA, A1, X1, D1, A2, RT, ZG, P3, U3, D2, CR, HX2, XX2, ZX2, GR1, ZGM, OT, HX1, ZX1, OM, GR0, ZGL,
 AG0, G1, G2, RS2, RS1, RS0) = tuple(range(22)) + tuple(range(22, 22 + 54, 9))
NSEM = 22 + 54
LATE = 5


def pieces(rows, period):
    out = {}
    for d in range(period):
        start = rows * d
        first = start // 128
        last = (start + rows - 1) // 128
        for b in range(first, last + 1):
            out.setdefault(b, []).append((d, b - first))
    return [out[b] for b in range(rows * period // 128)]


MID_PIECES = pieces(480, 4)
TOP_PIECES = pieces(240, 8)


def kernel(
    rhs0, rhs1, rhs2, outer, w0, q0, w1, q1, w2, q2, ltv, mtv, lt, mt, cnt,
    o_leaf, o_mid, o_top, o_con,
    wp0, wp1, wp2, qv0, qv1, qv2, at0, e, at, a, y0, y1, y2, le, sb1, lb1, sp1, rp1, c1, rm, sba1, la1, sb2, lb2, vm,
    s3p, r3p, s3u, r3u, rtq, sba2, la2, gtq, zt, ct, lc, g2, xpt, sbx, rbx, sby, ry, sz, lz, xs2, xx2, gm, gml, zm, lg1,
    g1, sbx1, rbx1, sby1, ry1, sz1, lz1, xsb1, gl, lg0, g0, sbl, ryl, szl, lzl, lot, lom,
    tmp, invv, inv, isem, wsem, ssem, rsem,
):
    s = lax.axis_index("leaf")
    r = lax.axis_index("rows")
    c = s % 2
    w4 = s % 4
    z = r // 4
    y = r % 4
    xb = (s // 2) % 2
    m1 = c * R + r
    m2 = w4 * R + r
    p1 = s + 1 - 2 * c
    p2 = s + 2 - 4 * xb
    p3 = p2 + 1 - 2 * c
    partners = (p1, p2, p3)

    barrier = pltpu.get_barrier_semaphore()

    def greet(k, _):
        pl.semaphore_signal(barrier, inc=1, device_id=(s, (r + k) % R), device_id_type=MESH)
        return 0

    lax.fori_loop(1, R, greet, 0)
    for p in partners:
        pl.semaphore_signal(barrier, inc=1, device_id=(p, r), device_id_type=MESH)

    off0 = pl.multiple_of((r % 2) * 64, 64)
    off1 = pl.multiple_of((r % 4) * 96 % 128, 32)
    off2 = pl.multiple_of((r % 8) * 112 % 128, 16)
    loads = []
    for k, (src, dst) in enumerate((
        (w0, wp0.at[pl.ds(off0, 960)]), (q0, qv0), (w1, wp1.at[pl.ds(off1, 480)]), (q1, qv1),
        (w2, wp2.at[pl.ds(off2, 240)]), (q2, qv2),
    )):
        copy = pltpu.make_async_copy(src, dst, wsem.at[k])
        copy.start()
        loads.append(copy)
    for wp, off, rows in ((wp0, off0, 960), (wp1, off1, 480), (wp2, off2, 240)):
        def zero_pad(t, _, wp=wp, off=off, rows=rows):
            at_row = jnp.where(16 * t < off, 16 * t, 16 * t + rows)
            wp[pl.ds(pl.multiple_of(at_row, 16), 16), :] = jnp.zeros((16, 2048), BF)
            return 0
        lax.fori_loop(0, (wp.shape[0] - rows) // 16, zero_pad, 0)
    zero_block = jnp.zeros((4, 128), BF)
    lb1[0] = zero_block
    vm[0] = zero_block
    vm[121] = zero_block
    ct[60] = zero_block
    zt[0:17] = jnp.zeros((17, 4, 128), BF)
    zm[0:17] = jnp.zeros((17, 4, 128), BF)
    gm[120] = zero_block

    piv0, piv1, piv2, upd2 = cnt[0, s], cnt[0, 8 + s // 2], cnt[0, 12 + s // 4], cnt[1, 12 + s // 4]

    def live(pivots, block):
        return jnp.clip(pivots - block * 128, 0, 1).astype(F32)

    f0, f1, f2 = live(piv0, r // 2), live(piv1, m1 // 4), live(piv2, m2 // 8)
    at0[...] = (rhs0[...].astype(F32) * f0).astype(BF)

    place = lax.broadcasted_iota(jnp.int32, (128, 128), 0)
    wanted = lax.broadcasted_iota(jnp.int32, (128, 128), 1)
    for row, (values, here) in enumerate(((ltv, s), (mtv, s // 2))):
        line = values[pl.ds(here, 1), :]
        parts = [line[:, :128], jnp.concatenate([line[:, 128:], jnp.full((1, 16), -1, jnp.int32)], axis=1)]
        found = [jnp.zeros((1, 128), jnp.int32)] * 2
        for k in range(2):
            target = jnp.broadcast_to(parts[k], (128, 128)).T
            j = place + 128 * k
            if row == 0:
                j = 1 + j + j // 15 + (j % 15 > 7).astype(jnp.int32)
            else:
                j = 1 + j
            for h in range(2):
                hit = jnp.where(target == wanted + 128 * h, j, 0)
                found[h] = found[h] + jnp.sum(hit, axis=0, keepdims=True)
        for h in range(2):
            invv[2 * row + h:2 * row + h + 1, :] = found[h]
    table = pltpu.make_async_copy(invv, inv, isem)
    table.start()

    def block_rows(x, rows, first):
        tmp[0:rows] = jnp.zeros((rows, 128), F32)
        tmp[pl.ds(pl.multiple_of(first, 16), x.shape[0]), :] = x
        return [tmp[b * 128:(b + 1) * 128].T for b in range(rows // 128)]

    e[:, 0] = block_rows(rhs1[...].astype(F32) * f1, 128, 32 * (r % 4))[0].reshape(R, 4, 128).astype(BF)
    e[:, 1] = block_rows(rhs2[...].astype(F32) * f2, 128, 16 * (r % 8))[0].reshape(R, 4, 128).astype(BF)
    row240 = lax.broadcasted_iota(jnp.int32, (240, 128), 0)
    given = jnp.where(row240 < upd2 - 240 * m2, outer[...].astype(F32), 0.0)
    for b, v in enumerate(block_rows(given, 384, off2)):
        g2[:, b * 128:(b + 1) * 128] = v.astype(BF)
        e[:, 2 + b] = v.reshape(R, 4, 128).astype(BF)

    pl.semaphore_wait(barrier, R - 1 + 3)

    landed = {}

    def remote(src, dst, n, dev, land):
        landed[n] = [land, False]
        return pltpu.make_async_remote_copy(
            src_ref=src, dst_ref=dst, send_sem=ssem.at[n], recv_sem=rsem.at[n], device_id=dev, device_id_type=MESH
        )

    def to_rows(src_of, dst, n, land):
        def send(k, _):
            d = (r + k) % R
            remote(src_of(d), dst, n, (s, d), land).start()
            return 0

        lax.fori_loop(1, R, send, 0)

    def arrived(n):
        ref = landed[n][0]
        landed[n][1] = True
        pltpu.make_async_copy(ref, ref, rsem.at[n]).wait()

    def sent(n):
        ref = landed[n][0]
        pltpu.make_async_copy(ref, ref, ssem.at[n]).wait()

    def to_early_rows(src_of, dst, n, land):
        def send(k, _):
            d = (r + k) % R

            @pl.when(d >= LATE)
            def _():
                remote(src_of(d), dst, n, (s, d), land).start()
            return 0

        lax.fori_loop(1, R, send, 0)

    def to_late_rows(src_of, dst, n, land):
        def send(d, _):
            @pl.when(d != r)
            def _():
                remote(src_of(d), dst, n, (s, d), land).start()
            return 0

        lax.fori_loop(0, LATE, send, 0)

    def gather(mine, dst, n, piece):
        def along_y(src, k):
            for j in (1, 3, 2):
                remote(src, dst(k), n, (s, z * 4 + (y + j) % 4), piece(24)).start()

        for k in (4, 3, 5, 2, 6, 1, 7):
            remote(mine, dst(r), n + k, (s, (z + k) % 8 * 4 + y), piece(1)).start()
        along_y(mine, r)
        for k in (1, 7, 2, 6, 3, 5, 4):
            arrived(n + k)
            other = (z + 8 - k) % 8 * 4 + y
            along_y(dst(other), other)
        arrived(n)

    def reduce_y(src, land, n, o, piece):
        t = (z + o) % 8
        for j in (1, 3, 2):
            remote(src(4 * t + (y + j) % 4), land.at[o, j - 1], n + o, (s, z * 4 + (y + j) % 4), piece(3)).start()

    def reduce_z(src, land, stage, final, n, o, piece):
        t = (z + o) % 8
        arrived(n + o)
        v = src[4 * t + y].astype(F32) + land[o, 0].astype(F32) + land[o, 1].astype(F32) + land[o, 2].astype(F32)
        if o == 0:
            return v
        stage[o - 1] = v.astype(BF)
        remote(stage.at[o - 1], final.at[o - 1], n + 8, (s, t * 4 + y), piece(7)).start()

    ORDER = (1, 2, 3, 4, 5, 6, 7, 0)

    def nt(x, w):
        return lax.dot_general(x, w, (((1,), (1,)), ((), ())), preferred_element_type=F32)

    at[r] = at0[...]
    gather(at0, lambda k: at.at[k], AG0, lambda k: at.at[pl.ds(0, k)])
    to_rows(lambda d: e.at[d], le.at[r], EA, le.at[pl.ds(0, R - 1)])
    le[r] = e[r]
    for k in range(16):
        block = at[2 * k:2 * k + 2].reshape(128, 128)
        a[:, k * 128:(k + 1) * 128] = block.T
    loads[0].wait()
    loads[1].wait()

    def leaf_update(t, _):
        prod = -nt(a[...], wp0[pl.ds(pl.multiple_of(t * 256, 256), 256), :])
        for b in range(2):
            sb1[:, 2 * t + b] = prod[:, b * 128:(b + 1) * 128].reshape(R, 4, 128).astype(BF)
        return 0

    lax.fori_loop(0, 4, leaf_update, 0)
    to_rows(lambda d: sb1.at[d], lb1.at[pl.ds(1 + r * 8, 8)], A1, lb1.at[pl.ds(0, 8 * (R - 1))])
    lb1[pl.ds(1 + r * 8, 8)] = sb1[r]
    y0[...] = (nt(a[...], qv0[...]) * f0).astype(BF)

    arrived(EA)
    for b in range(8):
        rm[b] = sum(le[4 * b + i, 0].astype(F32) for i in range(4))
    for b in range(4):
        rtq[4 * w4 + b] = sum(le[8 * b + i, 1].astype(F32) for i in range(8)).astype(BF)

    def outer_merge(q, _):
        for i, parts in enumerate(TOP_PIECES):
            v = sum(le[8 * q + d, 2 + k].astype(F32) for d, k in parts).astype(BF)
            gtq[15 * q + i] = v
            zt[17 + 60 * w4 + 15 * q + i] = v
        return 0

    lax.fori_loop(0, 4, outer_merge, 0)
    for p in partners:
        remote(rtq.at[pl.ds(4 * w4, 4)], rtq.at[pl.ds(4 * w4, 4)], RT, (p, r), rtq.at[pl.ds(0, 12)]).start()
        remote(gtq, zt.at[pl.ds(17 + 60 * w4, 60)], ZG, (p, r), zt.at[pl.ds(16, 180)]).start()
    loads[4].wait()
    loads[5].wait()

    def top_given(t, _):
        cols = pl.ds(pl.multiple_of(t * 256, 256), 256)
        xpt[:, cols] = -jnp.dot(g2[...], wp2[:, cols], preferred_element_type=F32)
        return 0

    lax.fori_loop(0, 8, top_given, 0)

    arrived(ZG)

    def mid_pick(j, _):
        v = zt[mt[s // 2, 120 * c + j] + 1]
        gm[j] = v
        zm[17 + 120 * c + j] = v
        return 0

    lax.fori_loop(0, 120, mid_pick, 0, unroll=8)
    for j in range(16, 20):
        gml[j] = gm[j]
    remote(gm.at[pl.ds(0, 120)], zm.at[pl.ds(17 + 120 * c, 120)], ZGM, (p1, r), zm.at[pl.ds(0, 120)]).start()

    arrived(A1)
    table.wait()

    def leaf_merge(q, _):
        lb1[16 * q + 8] = (lb1[16 * q + 8].astype(F32) + lb1[16 * q + 9].astype(F32)).astype(BF)
        return 0

    lax.fori_loop(0, 16, leaf_merge, 0)

    def child_block(core, j):
        b = jnp.where(j < 8, 8 * core, 8 + 120 * core) + j
        return jnp.clip(inv[b // 128, b % 128], 0, 256)

    def for_partner(j, _):
        sp1[j] = lb1[child_block(1 - c, j)]
        return 0

    lax.fori_loop(0, 128, for_partner, 0, unroll=8)
    remote(sp1, rp1, X1, (p1, r), rp1).start()

    def for_own(j, _):
        c1[j] = lb1[child_block(c, j)].astype(F32)
        return 0

    lax.fori_loop(0, 128, for_own, 0, unroll=8)
    arrived(X1)
    c1[...] = c1[...] + rp1[...].astype(F32)

    sba1[...] = (rm[...] + c1[0:8]).astype(BF)
    la1[c, r] = sba1[...]
    gather(sba1, lambda k: la1.at[c, k], G1, lambda k: la1.at[0, pl.ds(0, k)])
    remote(la1.at[c], la1.at[c], D1, (p1, r), la1.at[1 - c]).start()
    to_early_rows(lambda d: gm.at[pl.ds(480 * d // 128, 5)], lg1.at[r], GR1, lg1.at[pl.ds(0, R - 1)])
    lg1[r] = gm[pl.ds(480 * r // 128, 5)]
    arrived(D1)
    for h in range(2):
        for b in range(8):
            a[:, (8 * h + b) * 128:(8 * h + b + 1) * 128] = la1[h, :, b].reshape(128, 128)
    loads[2].wait()
    loads[3].wait()

    def mid_update(t, _):
        prod = nt(a[...], wp1[pl.ds(pl.multiple_of(t * 128, 128), 128), :])
        sb2[:, t] = prod.reshape(R, 4, 128).astype(BF)
        return 0

    lax.fori_loop(0, 5, mid_update, 0)
    to_rows(lambda d: sb2.at[d], lb2.at[r], A2, lb2.at[pl.ds(0, R - 1)])
    lb2[r] = sb2[r]
    y1[...] = (nt(a[...], qv1[...]) * f1).astype(BF)
    arrived(ZGM)

    def leaf_pick(j, _):
        gl[j] = zm[lt[s, j] + 1]
        return 0

    lax.fori_loop(32, 240, leaf_pick, 0, unroll=8)
    arrived(A2)
    to_early_rows(lambda d: gl.at[pl.ds(960 * d // 128, 8)], lg0.at[r], GR0, lg0.at[pl.ds(0, R - 1)])

    def mid_merge(q, _):
        for i, parts in enumerate(MID_PIECES):
            v = c1[8 + 15 * q + i] - sum(lb2[4 * q + d, k].astype(F32) for d, k in parts)
            vm[1 + 15 * q + i] = v.astype(BF)
        return 0

    lax.fori_loop(0, 8, mid_merge, 0)

    def parent_block(j):
        return jnp.clip(inv[2 + j // 128, j % 128] - 120 * c, 0, 121)

    for j in range(16):
        s3p[j] = vm[parent_block(j)]
    for k, p in enumerate(partners):
        remote(s3p, r3p.at[k], P3, (p, r), r3p).start()
    for k in range(3):
        def top_spread(j, _, k=k):
            s3u[k, j] = vm[parent_block(16 + 60 * (partners[k] % 4) + j)]
            return 0

        lax.fori_loop(0, 60, top_spread, 0, unroll=4)
        remote(s3u.at[k], r3u.at[k], U3, (partners[k], r), r3u).start()
    arrived(RT)
    arrived(P3)
    for j in range(16):
        v = rtq[j].astype(F32) + s3p[j].astype(F32) + sum(r3p[k, j].astype(F32) for k in range(3))
        sba2[j] = v.astype(BF)
    la2[c, r] = sba2[pl.ds(8 * c, 8)]
    gather(sba2.at[pl.ds(8 * c, 8)], lambda k: la2.at[c, k], G2, lambda k: la2.at[0, pl.ds(0, k)])
    arrived(U3)

    def top_sum(j, _):
        v = vm[parent_block(16 + 60 * w4 + j)].astype(F32) + sum(r3u[k, j].astype(F32) for k in range(3))
        ct[j] = v.astype(BF)
        return 0

    lax.fori_loop(0, 60, top_sum, 0, unroll=4)
    remote(la2.at[c], la2.at[c], D2, (p1, r), la2.at[1 - c]).start()
    to_rows(lambda d: ct.at[pl.ds(240 * d // 128, 3)], lc.at[r], CR, lc.at[pl.ds(0, R - 1)])
    lc[r] = ct[pl.ds(240 * r // 128, 3)]
    arrived(D2)
    for h in range(2):
        for b in range(8):
            a[:, (8 * h + b) * 128:(8 * h + b + 1) * 128] = la2[h, :, b].reshape(128, 128)
    y2[...] = (nt(a[...], qv2[...]) * f2).astype(BF)

    def top_partial(t, _):
        cols = pl.ds(pl.multiple_of(t * 256, 256), 256)
        v = xpt[:, cols] + jnp.dot(y2[...], qv2[:, cols], preferred_element_type=F32)
        for b in range(2):
            sbx[t // 4, :, 2 * (t % 4) + b] = v[:, b * 128:(b + 1) * 128].reshape(R, 4, 128).astype(BF)
        return 0

    lax.fori_loop(0, 8, top_partial, 0)
    remote(sbx.at[1 - c], rbx, HX2, (p1, r), rbx).start()
    prod = nt(a[...], wp2[...])
    arrived(CR)
    for b in range(3):
        v = lc[:, b].astype(F32).reshape(128, 128) - prod[:, b * 128:(b + 1) * 128]
        tmp[b * 128:(b + 1) * 128] = v.T
    o_con[...] = jnp.where(row240 < upd2 - 240 * m2, tmp[pl.ds(off2, 240), :], 0.0).astype(BF)
    arrived(HX2)

    def reduce_half(mine, other, both, land, stage, final, n):
        for o in ORDER:
            t = (z + o) % 8
            rows4 = pl.ds(4 * t, 4)
            both[rows4] = (mine[c, rows4].astype(F32) + other[rows4].astype(F32)).astype(BF)
            reduce_y(lambda d: both.at[d], land, n, o, lambda k: land.at[0, pl.ds(0, k)])
        for o in ORDER:
            v = reduce_z(both, land, stage, final, n, o, lambda k: final.at[pl.ds(0, k)])
        arrived(n + 8)
        for o in range(7):
            v = v + final[o].astype(F32)
        return v

    xs2[...] = reduce_half(sbx, rbx, sby, ry, sz, lz, RS2)
    remote(xs2, xx2, XX2, (p2, r), xx2).start()
    arrived(XX2)
    for b in range(8):
        zt[1 + 8 * c + b] = ((xs2[b] + xx2[b]) * live(piv2, 8 * c + b)).astype(BF)
    remote(zt.at[pl.ds(1 + 8 * c, 8)], zt.at[pl.ds(1 + 8 * c, 8)], ZX2, (p1, r), zt.at[pl.ds(0, 8)]).start()
    arrived(ZX2)

    for j in range(16):
        v = zt[mt[s // 2, 120 * c + j] + 1]
        gml[j] = v
        zm[17 + 120 * c + j] = v
    to_late_rows(lambda d: gml.at[pl.ds(480 * d // 128, 5)], lg1.at[r], GR1, lg1.at[pl.ds(0, R - 1)])

    @pl.when(r < LATE)
    def _():
        lg1[r] = gml[pl.ds(480 * jnp.minimum(r, LATE - 1) // 128, 5)]

    remote(gml.at[pl.ds(0, 16)], zm.at[pl.ds(17 + 120 * c, 16)], ZGL, (p1, r), zm.at[pl.ds(0, 16)]).start()
    to_rows(lambda d: zt.at[1 + 4 * w4 + d // 8], lot.at[r], OT, lot.at[pl.ds(0, R - 1)])
    lot[r] = zt[1 + 4 * w4 + r // 8]
    arrived(GR1)
    for b in range(5):
        g1[:, b * 128:(b + 1) * 128] = lg1[:, b].reshape(128, 128)

    def mid_partial(t, _):
        cols = pl.ds(pl.multiple_of(t * 256, 256), 256)
        v = jnp.dot(y1[...], qv1[:, cols], preferred_element_type=F32) - jnp.dot(
            g1[...], wp1[:, cols], preferred_element_type=F32
        )
        for b in range(2):
            sbx1[t // 4, :, 2 * (t % 4) + b] = v[:, b * 128:(b + 1) * 128].reshape(R, 4, 128).astype(BF)
        return 0

    lax.fori_loop(0, 8, mid_partial, 0)
    remote(sbx1.at[1 - c], rbx1, HX1, (p1, r), rbx1).start()
    arrived(HX1)
    xsum = reduce_half(sbx1, rbx1, sby1, ry1, sz1, lz1, RS1)
    for b in range(8):
        v = (xsum[b] * live(piv1, 8 * c + b)).astype(BF)
        xsb1[b] = v
        zm[1 + 8 * c + b] = v
    remote(xsb1, zm.at[pl.ds(1 + 8 * c, 8)], ZX1, (p1, r), zm.at[pl.ds(0, 8)]).start()
    arrived(ZX1)
    arrived(ZGL)

    lax.fori_loop(0, 32, leaf_pick, 0, unroll=8)
    to_late_rows(lambda d: gl.at[pl.ds(960 * d // 128, 8)], lg0.at[r], GR0, lg0.at[pl.ds(0, R - 1)])
    lg0[r] = gl[pl.ds(960 * r // 128, 8)]
    to_rows(lambda d: xsb1.at[d // 4], lom.at[r], OM, lom.at[pl.ds(0, R - 1)])
    lom[r] = xsb1[r // 4]
    arrived(OT)
    tmp[0:128] = lot[...].astype(F32).reshape(128, 128).T
    o_top[...] = tmp[pl.ds(pl.multiple_of(16 * (r % 8), 16), 16), :].astype(BF)
    arrived(GR0)
    for b in range(8):
        g0[:, b * 128:(b + 1) * 128] = lg0[:, b].reshape(128, 128)

    def leaf_tile(o):
        t = (z + o) % 8
        cols = pl.ds(pl.multiple_of(t * 256, 256), 256)
        v = jnp.dot(y0[...], qv0[:, cols], preferred_element_type=F32) - jnp.dot(
            g0[...], wp0[:, cols], preferred_element_type=F32
        )
        sbl[pl.ds(4 * t, 4)] = v.T.astype(BF).reshape(4, 64, 128)
        reduce_y(lambda d: sbl.at[d], ryl, RS0, o, lambda k: ryl.at[0, pl.ds(0, k)])

    def leaf_sum(o):
        return reduce_z(sbl, ryl, szl, lzl, RS0, o, lambda k: lzl.at[pl.ds(0, k)])

    for k in range(8):
        leaf_tile(ORDER[k])
        if k >= 3:
            leaf_sum(ORDER[k - 3])
    for k in range(5, 8):
        xl = leaf_sum(ORDER[k])
    arrived(OM)
    tmp[0:128] = lom[...].astype(F32).reshape(128, 128).T
    o_mid[...] = tmp[pl.ds(pl.multiple_of(32 * (r % 4), 32), 32), :].astype(BF)
    arrived(RS0 + 8)
    for o in range(7):
        xl = xl + lzl[o].astype(F32)
    o_leaf[...] = (xl * f0).astype(BF)

    for n in landed:
        sent(n)


SCRATCH = [
    ((1024, 2048), BF), ((640, 2048), BF), ((384, 2048), BF), ((64, 2048), BF), ((32, 2048), BF), ((16, 2048), BF),
    ((64, 128), BF), ((R, 5, 4, 128), BF),
    ((R, 64, 128), BF), ((128, 2048), BF), ((128, 64), BF), ((128, 32), BF), ((128, 16), BF), ((R, 5, 4, 128), BF),
    ((R, 8, 4, 128), BF), ((264, 4, 128), BF), ((128, 4, 128), BF), ((128, 4, 128), BF), ((128, 4, 128), F32),
    ((8, 4, 128), F32), ((8, 4, 128), BF), ((2, R, 8, 4, 128), BF), ((R, 5, 4, 128), BF), ((R, 5, 4, 128), BF),
    ((122, 4, 128), BF),
    ((16, 4, 128), BF), ((3, 16, 4, 128), BF), ((3, 60, 4, 128), BF), ((3, 60, 4, 128), BF), ((16, 4, 128), BF),
    ((16, 4, 128), BF), ((2, R, 8, 4, 128), BF), ((60, 4, 128), BF), ((257, 4, 128), BF), ((61, 4, 128), BF),
    ((R, 3, 4, 128), BF), ((128, 384), BF), ((128, 2048), F32), ((2, R, 8, 4, 128), BF), ((R, 8, 4, 128), BF),
    ((R, 8, 4, 128), BF), ((8, 3, 8, 4, 128), BF), ((7, 8, 4, 128), BF), ((7, 8, 4, 128), BF), ((8, 4, 128), F32), ((8, 4, 128), F32), ((121, 4, 128), BF), ((20, 4, 128), BF),
    ((257, 4, 128), BF), ((R, 5, 4, 128), BF), ((128, 640), BF),
    ((2, R, 8, 4, 128), BF), ((R, 8, 4, 128), BF), ((R, 8, 4, 128), BF), ((8, 3, 8, 4, 128), BF), ((7, 8, 4, 128), BF), ((7, 8, 4, 128), BF), ((8, 4, 128), BF),
    ((240, 4, 128), BF), ((R, 8, 4, 128), BF), ((128, 1024), BF), ((R, 64, 128), BF), ((8, 3, 64, 128), BF),
    ((7, 64, 128), BF), ((7, 64, 128), BF),
    ((R, 4, 128), BF), ((R, 4, 128), BF),
]


def hand_over(*refs):
    for k in range(4):
        refs[4 + k][...] = refs[k][...]


def body(
    leaf_inverse, leaf_panel, mid_inverse, mid_panel, top_inverse, top_panel,
    leaf_rhs, mid_rhs, top_rhs, outer_solution, leaf_targets, mid_targets, front_counts,
):
    vmem = pl.BlockSpec(memory_space=pltpu.VMEM)
    smem = pl.BlockSpec(memory_space=pltpu.SMEM)
    hbm = pl.BlockSpec(memory_space=pl.ANY)
    outs = pl.pallas_call(
        kernel,
        out_shape=tuple(jax.ShapeDtypeStruct((n, 128), BF) for n in (64, 32, 16, 240)),
        in_specs=[vmem] * 4 + [hbm] * 6 + [vmem] * 2 + [smem] * 3,
        out_specs=(vmem,) * 4,
        scratch_shapes=[pltpu.VMEM(shape, kind) for shape, kind in SCRATCH]
        + [pltpu.VMEM((384, 128), F32), pltpu.VMEM((8, 128), jnp.int32), pltpu.SMEM((8, 128), jnp.int32)]
        + [pltpu.SemaphoreType.DMA, pltpu.SemaphoreType.DMA((6,)), pltpu.SemaphoreType.DMA((NSEM,)), pltpu.SemaphoreType.DMA((NSEM,))],
        compiler_params=pltpu.CompilerParams(
            collective_id=0, has_side_effects=True, vmem_limit_bytes=56 * 1024 * 1024
        ),
        name="solve",
    )(
        leaf_rhs.T, mid_rhs.T, top_rhs.T, outer_solution.T,
        leaf_panel, leaf_inverse, mid_panel, mid_inverse, top_panel, top_inverse,
        leaf_targets, mid_targets, leaf_targets, mid_targets, front_counts.T,
    )
    shapes = tuple(jax.ShapeDtypeStruct(out.shape, BF) for out in outs)
    outs = pl.pallas_call(hand_over, out_shape=shapes, in_specs=[vmem] * 4, out_specs=(vmem,) * 4, name="hand_over")(*outs)
    return tuple(out.T for out in outs)


def solution(mesh):
    stacked = P(("leaf", "rows"), None)
    side = P(None, ("leaf", "rows"))
    return jax.shard_map(
        body,
        mesh=mesh,
        in_specs=(stacked,) * 6 + (side,) * 4 + (P(),) * 3,
        out_specs=(side,) * 4,
        check_vma=False,
    )
```

```python
import jax
import jax.numpy as jnp
from jax import lax
from jax.experimental import pallas as pl
from jax.experimental.pallas import tpu as pltpu
from jax.sharding import PartitionSpec as P

MESH = pl.DeviceIdType.MESH
BF = jnp.bfloat16
F32 = jnp.float32
R = 32

(EA, A1, X1, D1, A2, RT, ZG, P3, U3, D2, CR, HX2, XX2, ZX2, GR1, ZGM, OT, HX1, ZX1, OM, GR0, ZGL,
 AG0, G1, G2, RS2, RS1, RS0) = tuple(range(22)) + tuple(range(22, 22 + 54, 9))
NSEM = 22 + 54
LATE = 5


def pieces(rows, period):
    out = {}
    for d in range(period):
        start = rows * d
        first = start // 128
        last = (start + rows - 1) // 128
        for b in range(first, last + 1):
            out.setdefault(b, []).append((d, b - first))
    return [out[b] for b in range(rows * period // 128)]


MID_PIECES = pieces(480, 4)
TOP_PIECES = pieces(240, 8)


def kernel(
    rhs0, rhs1, rhs2, outer, w0, q0, w1, q1, w2, q2, ltv, mtv, lt, mt, cnt,
    o_leaf, o_mid, o_top, o_con,
    wp0, wp1, wp2, qv0, qv1, qv2, at0, e, at, a, y0, y1, y2, le, sb1, lb1, sp1, rp1, c1, rm, sba1, la1, sb2, lb2, vm,
    s3p, r3p, s3u, r3u, rtq, sba2, la2, gtq, zt, ct, lc, g2, xpt, sbx, rbx, sby, ry, sz, lz, xs2, xx2, gm, gml, zm, lg1,
    g1, sbx1, rbx1, sby1, ry1, sz1, lz1, xsb1, gl, lg0, g0, sbl, ryl, szl, lzl, lot, lom,
    tmp, invv, inv, isem, wsem, ssem, rsem,
):
    s = lax.axis_index("leaf")
    r = lax.axis_index("rows")
    c = s % 2
    w4 = s % 4
    z = r // 4
    y = r % 4
    xb = (s // 2) % 2
    m1 = c * R + r
    m2 = w4 * R + r
    p1 = s + 1 - 2 * c
    p2 = s + 2 - 4 * xb
    p3 = p2 + 1 - 2 * c
    partners = (p1, p2, p3)

    barrier = pltpu.get_barrier_semaphore()

    for k in range(1, 8):
        pl.semaphore_signal(barrier, inc=1, device_id=(s, (z + k) % 8 * 4 + y), device_id_type=MESH)
    for k in range(1, 4):
        pl.semaphore_signal(barrier, inc=1, device_id=(s, z * 4 + (y + k) % 4), device_id_type=MESH)
    for p in partners:
        pl.semaphore_signal(barrier, inc=1, device_id=(p, r), device_id_type=MESH)

    off0 = pl.multiple_of((r % 2) * 64, 64)
    off1 = pl.multiple_of((r % 4) * 96 % 128, 32)
    off2 = pl.multiple_of((r % 8) * 112 % 128, 16)
    loads = []
    for k, (src, dst) in enumerate((
        (w0, wp0.at[pl.ds(off0, 960)]), (q0, qv0), (w1, wp1.at[pl.ds(off1, 480)]), (q1, qv1),
        (w2, wp2.at[pl.ds(off2, 240)]), (q2, qv2),
    )):
        copy = pltpu.make_async_copy(src, dst, wsem.at[k])
        copy.start()
        loads.append(copy)
    for wp, off, rows in ((wp0, off0, 960), (wp1, off1, 480), (wp2, off2, 240)):
        def zero_pad(t, _, wp=wp, off=off, rows=rows):
            at_row = jnp.where(16 * t < off, 16 * t, 16 * t + rows)
            wp[pl.ds(pl.multiple_of(at_row, 16), 16), :] = jnp.zeros((16, 2048), BF)
            return 0
        lax.fori_loop(0, (wp.shape[0] - rows) // 16, zero_pad, 0)
    zero_block = jnp.zeros((4, 128), BF)
    lb1[0] = zero_block
    vm[0] = zero_block
    vm[121] = zero_block
    ct[60] = zero_block
    zt[0:17] = jnp.zeros((17, 4, 128), BF)
    zm[0:17] = jnp.zeros((17, 4, 128), BF)
    gm[120] = zero_block

    piv0, piv1, piv2, upd2 = cnt[0, s], cnt[0, 8 + s // 2], cnt[0, 12 + s // 4], cnt[1, 12 + s // 4]

    def live(pivots, block):
        return jnp.clip(pivots - block * 128, 0, 1).astype(F32)

    f0, f1, f2 = live(piv0, r // 2), live(piv1, m1 // 4), live(piv2, m2 // 8)
    at0[...] = (rhs0[...].astype(F32) * f0).astype(BF)

    place = lax.broadcasted_iota(jnp.int32, (128, 128), 0)
    wanted = lax.broadcasted_iota(jnp.int32, (128, 128), 1)
    for row, (values, here) in enumerate(((ltv, s), (mtv, s // 2))):
        line = values[pl.ds(here, 1), :]
        parts = [line[:, :128], jnp.concatenate([line[:, 128:], jnp.full((1, 16), -1, jnp.int32)], axis=1)]
        found = [jnp.zeros((1, 128), jnp.int32)] * 2
        for k in range(2):
            target = jnp.broadcast_to(parts[k], (128, 128)).T
            j = place + 128 * k
            if row == 0:
                j = 1 + j + j // 15 + (j % 15 > 7).astype(jnp.int32)
            else:
                j = 1 + j
            for h in range(2):
                hit = jnp.where(target == wanted + 128 * h, j, 0)
                found[h] = found[h] + jnp.sum(hit, axis=0, keepdims=True)
        for h in range(2):
            invv[2 * row + h:2 * row + h + 1, :] = found[h]
    table = pltpu.make_async_copy(invv, inv, isem)
    table.start()

    def block_rows(x, rows, first):
        tmp[0:rows] = jnp.zeros((rows, 128), F32)
        tmp[pl.ds(pl.multiple_of(first, 16), x.shape[0]), :] = x
        return [tmp[b * 128:(b + 1) * 128].T for b in range(rows // 128)]

    e[:, 0] = block_rows(rhs1[...].astype(F32) * f1, 128, 32 * (r % 4))[0].reshape(R, 4, 128).astype(BF)
    e[:, 1] = block_rows(rhs2[...].astype(F32) * f2, 128, 16 * (r % 8))[0].reshape(R, 4, 128).astype(BF)
    row240 = lax.broadcasted_iota(jnp.int32, (240, 128), 0)
    given = jnp.where(row240 < upd2 - 240 * m2, outer[...].astype(F32), 0.0)
    for b, v in enumerate(block_rows(given, 384, off2)):
        g2[:, b * 128:(b + 1) * 128] = v.astype(BF)
        e[:, 2 + b] = v.reshape(R, 4, 128).astype(BF)

    pl.semaphore_wait(barrier, 7 + 3 + 3)

    landed = {}

    def remote(src, dst, n, dev, land):
        landed[n] = [land, False]
        return pltpu.make_async_remote_copy(
            src_ref=src, dst_ref=dst, send_sem=ssem.at[n], recv_sem=rsem.at[n], device_id=dev, device_id_type=MESH
        )

    def to_rows(src_of, dst, n, land):
        def send(k, _):
            d = (r + k) % R
            remote(src_of(d), dst, n, (s, d), land).start()
            return 0

        lax.fori_loop(1, R, send, 0)

    def arrived(n):
        ref = landed[n][0]
        landed[n][1] = True
        pltpu.make_async_copy(ref, ref, rsem.at[n]).wait()

    def sent(n):
        ref = landed[n][0]
        pltpu.make_async_copy(ref, ref, ssem.at[n]).wait()

    def to_early_rows(src_of, dst, n, land):
        def send(k, _):
            d = (r + k) % R

            @pl.when(d >= LATE)
            def _():
                remote(src_of(d), dst, n, (s, d), land).start()
            return 0

        lax.fori_loop(1, R, send, 0)

    def to_late_rows(src_of, dst, n, land):
        def send(d, _):
            @pl.when(d != r)
            def _():
                remote(src_of(d), dst, n, (s, d), land).start()
            return 0

        lax.fori_loop(0, LATE, send, 0)

    def gather(mine, dst, n, piece):
        def along_y(src, k):
            for j in (1, 3, 2):
                remote(src, dst(k), n, (s, z * 4 + (y + j) % 4), piece(24)).start()

        for k in (4, 3, 5, 2, 6, 1, 7):
            remote(mine, dst(r), n + k, (s, (z + k) % 8 * 4 + y), piece(1)).start()
        along_y(mine, r)
        for k in (1, 7, 2, 6, 3, 5, 4):
            arrived(n + k)
            other = (z + 8 - k) % 8 * 4 + y
            along_y(dst(other), other)
        arrived(n)

    def reduce_y(src, land, n, o, piece):
        t = (z + o) % 8
        for j in (1, 3, 2):
            remote(src(4 * t + (y + j) % 4), land.at[o, j - 1], n + o, (s, z * 4 + (y + j) % 4), piece(3)).start()

    def reduce_z(src, land, stage, final, n, o, piece):
        t = (z + o) % 8
        arrived(n + o)
        v = src[4 * t + y].astype(F32) + land[o, 0].astype(F32) + land[o, 1].astype(F32) + land[o, 2].astype(F32)
        if o == 0:
            return v
        stage[o - 1] = v.astype(BF)
        remote(stage.at[o - 1], final.at[o - 1], n + 8, (s, t * 4 + y), piece(7)).start()

    ORDER = (4, 3, 5, 2, 6, 1, 7, 0)

    def nt(x, w):
        return lax.dot_general(x, w, (((1,), (1,)), ((), ())), preferred_element_type=F32)

    at[r] = at0[...]
    gather(at0, lambda k: at.at[k], AG0, lambda k: at.at[pl.ds(0, k)])
    to_rows(lambda d: e.at[d], le.at[r], EA, le.at[pl.ds(0, R - 1)])
    le[r] = e[r]
    for k in range(16):
        block = at[2 * k:2 * k + 2].reshape(128, 128)
        a[:, k * 128:(k + 1) * 128] = block.T
    loads[0].wait()
    loads[1].wait()

    def leaf_update(t, _):
        prod = -nt(a[...], wp0[pl.ds(pl.multiple_of(t * 256, 256), 256), :])
        for b in range(2):
            sb1[:, 2 * t + b] = prod[:, b * 128:(b + 1) * 128].reshape(R, 4, 128).astype(BF)
        return 0

    lax.fori_loop(0, 4, leaf_update, 0)
    to_rows(lambda d: sb1.at[d], lb1.at[pl.ds(1 + r * 8, 8)], A1, lb1.at[pl.ds(0, 8 * (R - 1))])
    lb1[pl.ds(1 + r * 8, 8)] = sb1[r]
    y0[...] = (nt(a[...], qv0[...]) * f0).astype(BF)

    arrived(EA)
    for b in range(8):
        rm[b] = sum(le[4 * b + i, 0].astype(F32) for i in range(4))
    for b in range(4):
        rtq[4 * w4 + b] = sum(le[8 * b + i, 1].astype(F32) for i in range(8)).astype(BF)

    def outer_merge(q, _):
        for i, parts in enumerate(TOP_PIECES):
            v = sum(le[8 * q + d, 2 + k].astype(F32) for d, k in parts).astype(BF)
            gtq[15 * q + i] = v
            zt[17 + 60 * w4 + 15 * q + i] = v
        return 0

    lax.fori_loop(0, 4, outer_merge, 0)
    for p in partners:
        remote(rtq.at[pl.ds(4 * w4, 4)], rtq.at[pl.ds(4 * w4, 4)], RT, (p, r), rtq.at[pl.ds(0, 12)]).start()
        remote(gtq, zt.at[pl.ds(17 + 60 * w4, 60)], ZG, (p, r), zt.at[pl.ds(16, 180)]).start()
    loads[4].wait()
    loads[5].wait()

    def top_given(t, _):
        cols = pl.ds(pl.multiple_of(t * 256, 256), 256)
        xpt[:, cols] = -jnp.dot(g2[...], wp2[:, cols], preferred_element_type=F32)
        return 0

    lax.fori_loop(0, 8, top_given, 0)

    arrived(ZG)

    def mid_pick(j, _):
        v = zt[mt[s // 2, 120 * c + j] + 1]
        gm[j] = v
        zm[17 + 120 * c + j] = v
        return 0

    lax.fori_loop(0, 120, mid_pick, 0, unroll=8)
    for j in range(16, 20):
        gml[j] = gm[j]
    remote(gm.at[pl.ds(0, 120)], zm.at[pl.ds(17 + 120 * c, 120)], ZGM, (p1, r), zm.at[pl.ds(0, 120)]).start()

    arrived(A1)
    table.wait()

    def leaf_merge(q, _):
        lb1[16 * q + 8] = (lb1[16 * q + 8].astype(F32) + lb1[16 * q + 9].astype(F32)).astype(BF)
        return 0

    lax.fori_loop(0, 16, leaf_merge, 0)

    def child_block(core, j):
        b = jnp.where(j < 8, 8 * core, 8 + 120 * core) + j
        return jnp.clip(inv[b // 128, b % 128], 0, 256)

    def for_partner(j, _):
        sp1[j] = lb1[child_block(1 - c, j)]
        return 0

    lax.fori_loop(0, 128, for_partner, 0, unroll=8)
    remote(sp1, rp1, X1, (p1, r), rp1).start()

    def for_own(j, _):
        c1[j] = lb1[child_block(c, j)].astype(F32)
        return 0

    lax.fori_loop(0, 128, for_own, 0, unroll=8)
    arrived(X1)
    c1[...] = c1[...] + rp1[...].astype(F32)

    sba1[...] = (rm[...] + c1[0:8]).astype(BF)
    la1[c, r] = sba1[...]
    gather(sba1, lambda k: la1.at[c, k], G1, lambda k: la1.at[0, pl.ds(0, k)])
    remote(la1.at[c], la1.at[c], D1, (p1, r), la1.at[1 - c]).start()
    to_early_rows(lambda d: gm.at[pl.ds(480 * d // 128, 5)], lg1.at[r], GR1, lg1.at[pl.ds(0, R - 1)])
    lg1[r] = gm[pl.ds(480 * r // 128, 5)]
    arrived(D1)
    for h in range(2):
        for b in range(8):
            a[:, (8 * h + b) * 128:(8 * h + b + 1) * 128] = la1[h, :, b].reshape(128, 128)
    loads[2].wait()
    loads[3].wait()

    for t in range(0, 5, 2):
        prod = nt(a[...], wp1[t * 128:min(t + 2, 5) * 128, :])
        for b in range(t, min(t + 2, 5)):
            sb2[:, b] = prod[:, (b - t) * 128:(b - t + 1) * 128].reshape(R, 4, 128).astype(BF)
    to_rows(lambda d: sb2.at[d], lb2.at[r], A2, lb2.at[pl.ds(0, R - 1)])
    lb2[r] = sb2[r]
    y1[...] = (nt(a[...], qv1[...]) * f1).astype(BF)
    arrived(ZGM)

    def leaf_pick(j, _):
        gl[j] = zm[lt[s, j] + 1]
        return 0

    lax.fori_loop(32, 240, leaf_pick, 0, unroll=8)
    arrived(A2)
    to_early_rows(lambda d: gl.at[pl.ds(960 * d // 128, 8)], lg0.at[r], GR0, lg0.at[pl.ds(0, R - 1)])

    def mid_merge(q, _):
        for i, parts in enumerate(MID_PIECES):
            v = c1[8 + 15 * q + i] - sum(lb2[4 * q + d, k].astype(F32) for d, k in parts)
            vm[1 + 15 * q + i] = v.astype(BF)
        return 0

    lax.fori_loop(0, 8, mid_merge, 0)

    def parent_block(j):
        return jnp.clip(inv[2 + j // 128, j % 128] - 120 * c, 0, 121)

    for j in range(16):
        s3p[j] = vm[parent_block(j)]
    for k, p in enumerate(partners):
        remote(s3p, r3p.at[k], P3, (p, r), r3p).start()
    for k in range(3):
        def top_spread(j, _, k=k):
            s3u[k, j] = vm[parent_block(16 + 60 * (partners[k] % 4) + j)]
            return 0

        lax.fori_loop(0, 60, top_spread, 0, unroll=4)
        remote(s3u.at[k], r3u.at[k], U3, (partners[k], r), r3u).start()
    arrived(RT)
    arrived(P3)
    for j in range(16):
        v = rtq[j].astype(F32) + s3p[j].astype(F32) + sum(r3p[k, j].astype(F32) for k in range(3))
        sba2[j] = v.astype(BF)
    la2[c, r] = sba2[pl.ds(8 * c, 8)]
    gather(sba2.at[pl.ds(8 * c, 8)], lambda k: la2.at[c, k], G2, lambda k: la2.at[0, pl.ds(0, k)])
    arrived(U3)

    def top_sum(j, _):
        v = vm[parent_block(16 + 60 * w4 + j)].astype(F32) + sum(r3u[k, j].astype(F32) for k in range(3))
        ct[j] = v.astype(BF)
        return 0

    lax.fori_loop(0, 60, top_sum, 0, unroll=4)
    remote(la2.at[c], la2.at[c], D2, (p1, r), la2.at[1 - c]).start()
    to_rows(lambda d: ct.at[pl.ds(240 * d // 128, 3)], lc.at[r], CR, lc.at[pl.ds(0, R - 1)])
    lc[r] = ct[pl.ds(240 * r // 128, 3)]
    arrived(D2)
    for h in range(2):
        for b in range(8):
            a[:, (8 * h + b) * 128:(8 * h + b + 1) * 128] = la2[h, :, b].reshape(128, 128)
    y2[...] = (nt(a[...], qv2[...]) * f2).astype(BF)

    def top_partial(t, _):
        cols = pl.ds(pl.multiple_of(t * 256, 256), 256)
        v = xpt[:, cols] + jnp.dot(y2[...], qv2[:, cols], preferred_element_type=F32)
        for b in range(2):
            sbx[t // 4, :, 2 * (t % 4) + b] = v[:, b * 128:(b + 1) * 128].reshape(R, 4, 128).astype(BF)
        return 0

    lax.fori_loop(0, 8, top_partial, 0)
    remote(sbx.at[1 - c], rbx, HX2, (p1, r), rbx).start()
    prod = nt(a[...], wp2[...])
    arrived(CR)
    for b in range(3):
        v = lc[:, b].astype(F32).reshape(128, 128) - prod[:, b * 128:(b + 1) * 128]
        tmp[b * 128:(b + 1) * 128] = v.T
    o_con[...] = jnp.where(row240 < upd2 - 240 * m2, tmp[pl.ds(off2, 240), :], 0.0).astype(BF)
    arrived(HX2)

    def reduce_half(mine, other, both, land, stage, final, n):
        for o in ORDER:
            t = (z + o) % 8
            rows4 = pl.ds(4 * t, 4)
            both[rows4] = (mine[c, rows4].astype(F32) + other[rows4].astype(F32)).astype(BF)
            reduce_y(lambda d: both.at[d], land, n, o, lambda k: land.at[0, pl.ds(0, k)])
        for o in ORDER:
            v = reduce_z(both, land, stage, final, n, o, lambda k: final.at[pl.ds(0, k)])
        arrived(n + 8)
        for o in range(7):
            v = v + final[o].astype(F32)
        return v

    xs2[...] = reduce_half(sbx, rbx, sby, ry, sz, lz, RS2)
    remote(xs2, xx2, XX2, (p2, r), xx2).start()
    arrived(XX2)
    for b in range(8):
        zt[1 + 8 * c + b] = ((xs2[b] + xx2[b]) * live(piv2, 8 * c + b)).astype(BF)
    remote(zt.at[pl.ds(1 + 8 * c, 8)], zt.at[pl.ds(1 + 8 * c, 8)], ZX2, (p1, r), zt.at[pl.ds(0, 8)]).start()
    arrived(ZX2)

    for j in range(16):
        v = zt[mt[s // 2, 120 * c + j] + 1]
        gml[j] = v
        zm[17 + 120 * c + j] = v
    to_late_rows(lambda d: gml.at[pl.ds(480 * d // 128, 5)], lg1.at[r], GR1, lg1.at[pl.ds(0, R - 1)])

    @pl.when(r < LATE)
    def _():
        lg1[r] = gml[pl.ds(480 * jnp.minimum(r, LATE - 1) // 128, 5)]

    remote(gml.at[pl.ds(0, 16)], zm.at[pl.ds(17 + 120 * c, 16)], ZGL, (p1, r), zm.at[pl.ds(0, 16)]).start()
    to_rows(lambda d: zt.at[1 + 4 * w4 + d // 8], lot.at[r], OT, lot.at[pl.ds(0, R - 1)])
    lot[r] = zt[1 + 4 * w4 + r // 8]
    arrived(GR1)
    for b in range(5):
        g1[:, b * 128:(b + 1) * 128] = lg1[:, b].reshape(128, 128)

    def mid_partial(t, _):
        cols = pl.ds(pl.multiple_of(t * 256, 256), 256)
        v = jnp.dot(y1[...], qv1[:, cols], preferred_element_type=F32) - jnp.dot(
            g1[...], wp1[:, cols], preferred_element_type=F32
        )
        for b in range(2):
            sbx1[t // 4, :, 2 * (t % 4) + b] = v[:, b * 128:(b + 1) * 128].reshape(R, 4, 128).astype(BF)
        return 0

    lax.fori_loop(0, 8, mid_partial, 0)
    remote(sbx1.at[1 - c], rbx1, HX1, (p1, r), rbx1).start()
    arrived(HX1)
    xsum = reduce_half(sbx1, rbx1, sby1, ry1, sz1, lz1, RS1)
    for b in range(8):
        v = (xsum[b] * live(piv1, 8 * c + b)).astype(BF)
        xsb1[b] = v
        zm[1 + 8 * c + b] = v
    remote(xsb1, zm.at[pl.ds(1 + 8 * c, 8)], ZX1, (p1, r), zm.at[pl.ds(0, 8)]).start()
    arrived(ZX1)
    arrived(ZGL)

    lax.fori_loop(0, 32, leaf_pick, 0, unroll=8)
    to_late_rows(lambda d: gl.at[pl.ds(960 * d // 128, 8)], lg0.at[r], GR0, lg0.at[pl.ds(0, R - 1)])
    lg0[r] = gl[pl.ds(960 * r // 128, 8)]
    to_rows(lambda d: xsb1.at[d // 4], lom.at[r], OM, lom.at[pl.ds(0, R - 1)])
    lom[r] = xsb1[r // 4]
    arrived(OT)
    tmp[0:128] = lot[...].astype(F32).reshape(128, 128).T
    o_top[...] = tmp[pl.ds(pl.multiple_of(16 * (r % 8), 16), 16), :].astype(BF)
    arrived(GR0)
    for b in range(8):
        g0[:, b * 128:(b + 1) * 128] = lg0[:, b].reshape(128, 128)

    def leaf_tile(o):
        t = (z + o) % 8
        cols = pl.ds(pl.multiple_of(t * 256, 256), 256)
        v = jnp.dot(y0[...], qv0[:, cols], preferred_element_type=F32) - jnp.dot(
            g0[...], wp0[:, cols], preferred_element_type=F32
        )
        sbl[pl.ds(4 * t, 4)] = v.T.astype(BF).reshape(4, 64, 128)
        reduce_y(lambda d: sbl.at[d], ryl, RS0, o, lambda k: ryl.at[0, pl.ds(0, k)])

    def leaf_sum(o):
        return reduce_z(sbl, ryl, szl, lzl, RS0, o, lambda k: lzl.at[pl.ds(0, k)])

    for k in range(8):
        leaf_tile(ORDER[k])
        if k >= 4:
            leaf_sum(ORDER[k - 4])
    for k in range(4, 8):
        xl = leaf_sum(ORDER[k])
    arrived(OM)
    tmp[0:128] = lom[...].astype(F32).reshape(128, 128).T
    o_mid[...] = tmp[pl.ds(pl.multiple_of(32 * (r % 4), 32), 32), :].astype(BF)
    arrived(RS0 + 8)
    for o in range(7):
        xl = xl + lzl[o].astype(F32)
    o_leaf[...] = (xl * f0).astype(BF)

    for n in landed:
        sent(n)


SCRATCH = [
    ((1024, 2048), BF), ((640, 2048), BF), ((384, 2048), BF), ((64, 2048), BF), ((32, 2048), BF), ((16, 2048), BF),
    ((64, 128), BF), ((R, 5, 4, 128), BF),
    ((R, 64, 128), BF), ((128, 2048), BF), ((128, 64), BF), ((128, 32), BF), ((128, 16), BF), ((R, 5, 4, 128), BF),
    ((R, 8, 4, 128), BF), ((264, 4, 128), BF), ((128, 4, 128), BF), ((128, 4, 128), BF), ((128, 4, 128), F32),
    ((8, 4, 128), F32), ((8, 4, 128), BF), ((2, R, 8, 4, 128), BF), ((R, 5, 4, 128), BF), ((R, 5, 4, 128), BF),
    ((122, 4, 128), BF),
    ((16, 4, 128), BF), ((3, 16, 4, 128), BF), ((3, 60, 4, 128), BF), ((3, 60, 4, 128), BF), ((16, 4, 128), BF),
    ((16, 4, 128), BF), ((2, R, 8, 4, 128), BF), ((60, 4, 128), BF), ((257, 4, 128), BF), ((61, 4, 128), BF),
    ((R, 3, 4, 128), BF), ((128, 384), BF), ((128, 2048), F32), ((2, R, 8, 4, 128), BF), ((R, 8, 4, 128), BF),
    ((R, 8, 4, 128), BF), ((8, 3, 8, 4, 128), BF), ((7, 8, 4, 128), BF), ((7, 8, 4, 128), BF), ((8, 4, 128), F32), ((8, 4, 128), F32), ((121, 4, 128), BF), ((20, 4, 128), BF),
    ((257, 4, 128), BF), ((R, 5, 4, 128), BF), ((128, 640), BF),
    ((2, R, 8, 4, 128), BF), ((R, 8, 4, 128), BF), ((R, 8, 4, 128), BF), ((8, 3, 8, 4, 128), BF), ((7, 8, 4, 128), BF), ((7, 8, 4, 128), BF), ((8, 4, 128), BF),
    ((240, 4, 128), BF), ((R, 8, 4, 128), BF), ((128, 1024), BF), ((R, 64, 128), BF), ((8, 3, 64, 128), BF),
    ((7, 64, 128), BF), ((7, 64, 128), BF),
    ((R, 4, 128), BF), ((R, 4, 128), BF),
]


def hand_over(*refs):
    for k in range(4):
        refs[4 + k][...] = refs[k][...]


def body(
    leaf_inverse, leaf_panel, mid_inverse, mid_panel, top_inverse, top_panel,
    leaf_rhs, mid_rhs, top_rhs, outer_solution, leaf_targets, mid_targets, front_counts,
):
    vmem = pl.BlockSpec(memory_space=pltpu.VMEM)
    smem = pl.BlockSpec(memory_space=pltpu.SMEM)
    hbm = pl.BlockSpec(memory_space=pl.ANY)
    outs = pl.pallas_call(
        kernel,
        out_shape=tuple(jax.ShapeDtypeStruct((n, 128), BF) for n in (64, 32, 16, 240)),
        in_specs=[vmem] * 4 + [hbm] * 6 + [vmem] * 2 + [smem] * 3,
        out_specs=(vmem,) * 4,
        scratch_shapes=[pltpu.VMEM(shape, kind) for shape, kind in SCRATCH]
        + [pltpu.VMEM((384, 128), F32), pltpu.VMEM((8, 128), jnp.int32), pltpu.SMEM((8, 128), jnp.int32)]
        + [pltpu.SemaphoreType.DMA, pltpu.SemaphoreType.DMA((6,)), pltpu.SemaphoreType.DMA((NSEM,)), pltpu.SemaphoreType.DMA((NSEM,))],
        compiler_params=pltpu.CompilerParams(
            collective_id=0, has_side_effects=True, vmem_limit_bytes=56 * 1024 * 1024
        ),
        name="solve",
    )(
        leaf_rhs.T, mid_rhs.T, top_rhs.T, outer_solution.T,
        leaf_panel, leaf_inverse, mid_panel, mid_inverse, top_panel, top_inverse,
        leaf_targets, mid_targets, leaf_targets, mid_targets, front_counts.T,
    )
    shapes = tuple(jax.ShapeDtypeStruct(out.shape, BF) for out in outs)
    outs = pl.pallas_call(hand_over, out_shape=shapes, in_specs=[vmem] * 4, out_specs=(vmem,) * 4, name="hand_over")(*outs)
    return tuple(out.T for out in outs)


def solution(mesh):
    stacked = P(("leaf", "rows"), None)
    side = P(None, ("leaf", "rows"))
    return jax.shard_map(
        body,
        mesh=mesh,
        in_specs=(stacked,) * 6 + (side,) * 4 + (P(),) * 3,
        out_specs=(side,) * 4,
        check_vma=False,
    )
```

```python
import jax
import jax.numpy as jnp
from jax import lax
from jax.experimental import pallas as pl
from jax.experimental.pallas import tpu as pltpu
from jax.sharding import PartitionSpec as P

MESH = pl.DeviceIdType.MESH
BF = jnp.bfloat16
F32 = jnp.float32
R = 32

(EA, A1, X1, D1, A2, RT, ZG, P3, U3, D2, CR, HX2, XX2, ZX2, GR1, ZGM, OT, HX1, ZX1, OM, GR0, ZGL,
 AG0, G1, G2, RS2, RS1, RS0) = tuple(range(22)) + tuple(range(22, 22 + 54, 9))
NSEM = 22 + 54
LATE = 5


def pieces(rows, period):
    out = {}
    for d in range(period):
        start = rows * d
        first = start // 128
        last = (start + rows - 1) // 128
        for b in range(first, last + 1):
            out.setdefault(b, []).append((d, b - first))
    return [out[b] for b in range(rows * period // 128)]


MID_PIECES = pieces(480, 4)
TOP_PIECES = pieces(240, 8)


def kernel(
    rhs0, rhs1, rhs2, outer, w0, q0, w1, q1, w2, q2, ltv, mtv, lt, mt, cnt,
    o_leaf, o_mid, o_top, o_con,
    wp0, wp1, wp2, qv0, qv1, qv2, at0, e, at, a, y0, y1, y2, le, sb1, lb1, sp1, rp1, c1, rm, sba1, la1, sb2, lb2, vm,
    s3p, r3p, s3u, r3u, rtq, sba2, la2, gtq, zt, ct, lc, g2, xpt, sbx, rbx, sby, ry, sz, lz, xs2, xx2, gm, gml, zm, lg1,
    g1, sbx1, rbx1, sby1, ry1, sz1, lz1, xsb1, gl, lg0, g0, sbl, ryl, szl, lzl, lot, lom,
    tmp, invv, inv, isem, wsem, ssem, rsem,
):
    s = lax.axis_index("leaf")
    r = lax.axis_index("rows")
    c = s % 2
    w4 = s % 4
    z = r // 4
    y = r % 4
    xb = (s // 2) % 2
    m1 = c * R + r
    m2 = w4 * R + r
    p1 = s + 1 - 2 * c
    p2 = s + 2 - 4 * xb
    p3 = p2 + 1 - 2 * c
    partners = (p1, p2, p3)

    barrier = pltpu.get_barrier_semaphore()

    for k in range(1, 8):
        pl.semaphore_signal(barrier, inc=1, device_id=(s, (z + k) % 8 * 4 + y), device_id_type=MESH)
    for k in range(1, 4):
        pl.semaphore_signal(barrier, inc=1, device_id=(s, z * 4 + (y + k) % 4), device_id_type=MESH)
    for p in partners:
        pl.semaphore_signal(barrier, inc=1, device_id=(p, r), device_id_type=MESH)

    off0 = pl.multiple_of((r % 2) * 64, 64)
    off1 = pl.multiple_of((r % 4) * 96 % 128, 32)
    off2 = pl.multiple_of((r % 8) * 112 % 128, 16)
    loads = []
    for k, (src, dst) in enumerate((
        (w0, wp0.at[pl.ds(off0, 960)]), (q0, qv0), (w1, wp1.at[pl.ds(off1, 480)]), (q1, qv1),
        (w2, wp2.at[pl.ds(off2, 240)]), (q2, qv2),
    )):
        copy = pltpu.make_async_copy(src, dst, wsem.at[k])
        copy.start()
        loads.append(copy)
    for wp, off, rows in ((wp0, off0, 960), (wp1, off1, 480), (wp2, off2, 240)):
        def zero_pad(t, _, wp=wp, off=off, rows=rows):
            at_row = jnp.where(16 * t < off, 16 * t, 16 * t + rows)
            wp[pl.ds(pl.multiple_of(at_row, 16), 16), :] = jnp.zeros((16, 2048), BF)
            return 0
        lax.fori_loop(0, (wp.shape[0] - rows) // 16, zero_pad, 0)
    zero_block = jnp.zeros((4, 128), BF)
    lb1[0] = zero_block
    vm[0] = zero_block
    vm[121] = zero_block
    ct[60] = zero_block
    zt[0:17] = jnp.zeros((17, 4, 128), BF)
    zm[0:17] = jnp.zeros((17, 4, 128), BF)
    gm[120] = zero_block

    piv0, piv1, piv2, upd2 = cnt[0, s], cnt[0, 8 + s // 2], cnt[0, 12 + s // 4], cnt[1, 12 + s // 4]

    def live(pivots, block):
        return jnp.clip(pivots - block * 128, 0, 1).astype(F32)

    f0, f1, f2 = live(piv0, r // 2), live(piv1, m1 // 4), live(piv2, m2 // 8)
    at0[...] = (rhs0[...].astype(F32) * f0).astype(BF)

    place = lax.broadcasted_iota(jnp.int32, (128, 128), 0)
    wanted = lax.broadcasted_iota(jnp.int32, (128, 128), 1)
    for row, (values, here) in enumerate(((ltv, s), (mtv, s // 2))):
        line = values[pl.ds(here, 1), :]
        parts = [line[:, :128], jnp.concatenate([line[:, 128:], jnp.full((1, 16), -1, jnp.int32)], axis=1)]
        found = [jnp.zeros((1, 128), jnp.int32)] * 2
        for k in range(2):
            target = jnp.broadcast_to(parts[k], (128, 128)).T
            j = place + 128 * k
            if row == 0:
                j = 1 + j + j // 15 + (j % 15 > 7).astype(jnp.int32)
            else:
                j = 1 + j
            for h in range(2):
                hit = jnp.where(target == wanted + 128 * h, j, 0)
                found[h] = found[h] + jnp.sum(hit, axis=0, keepdims=True)
        for h in range(2):
            invv[2 * row + h:2 * row + h + 1, :] = found[h]
    table = pltpu.make_async_copy(invv, inv, isem)
    table.start()

    def block_rows(x, rows, first):
        tmp[0:rows] = jnp.zeros((rows, 128), F32)
        tmp[pl.ds(pl.multiple_of(first, 16), x.shape[0]), :] = x
        return [tmp[b * 128:(b + 1) * 128].T for b in range(rows // 128)]

    e[:, 0] = block_rows(rhs1[...].astype(F32) * f1, 128, 32 * (r % 4))[0].reshape(R, 4, 128).astype(BF)
    e[:, 1] = block_rows(rhs2[...].astype(F32) * f2, 128, 16 * (r % 8))[0].reshape(R, 4, 128).astype(BF)
    row240 = lax.broadcasted_iota(jnp.int32, (240, 128), 0)
    given = jnp.where(row240 < upd2 - 240 * m2, outer[...].astype(F32), 0.0)
    for b, v in enumerate(block_rows(given, 384, off2)):
        g2[:, b * 128:(b + 1) * 128] = v.astype(BF)
        e[:, 2 + b] = v.reshape(R, 4, 128).astype(BF)

    pl.semaphore_wait(barrier, 7 + 3 + 3)

    landed = {}

    def remote(src, dst, n, dev, land):
        landed[n] = [land, False]
        return pltpu.make_async_remote_copy(
            src_ref=src, dst_ref=dst, send_sem=ssem.at[n], recv_sem=rsem.at[n], device_id=dev, device_id_type=MESH
        )

    def to_rows(src_of, dst, n, land):
        def send(k, _):
            d = (r + k) % R
            remote(src_of(d), dst, n, (s, d), land).start()
            return 0

        lax.fori_loop(1, R, send, 0)

    def arrived(n):
        ref = landed[n][0]
        landed[n][1] = True
        pltpu.make_async_copy(ref, ref, rsem.at[n]).wait()

    def sent(n):
        ref = landed[n][0]
        pltpu.make_async_copy(ref, ref, ssem.at[n]).wait()

    def to_early_rows(src_of, dst, n, land):
        def send(k, _):
            d = (r + k) % R

            @pl.when(d >= LATE)
            def _():
                remote(src_of(d), dst, n, (s, d), land).start()
            return 0

        lax.fori_loop(1, R, send, 0)

    def to_late_rows(src_of, dst, n, land):
        def send(d, _):
            @pl.when(d != r)
            def _():
                remote(src_of(d), dst, n, (s, d), land).start()
            return 0

        lax.fori_loop(0, LATE, send, 0)

    def gather(mine, dst, n, piece):
        def along_y(src, k):
            for j in (1, 3, 2):
                remote(src, dst(k), n, (s, z * 4 + (y + j) % 4), piece(24)).start()

        for k in (4, 3, 5, 2, 6, 1, 7):
            remote(mine, dst(r), n + k, (s, (z + k) % 8 * 4 + y), piece(1)).start()
        along_y(mine, r)
        for k in (1, 7, 2, 6, 3, 5, 4):
            arrived(n + k)
            other = (z + 8 - k) % 8 * 4 + y
            along_y(dst(other), other)
        arrived(n)

    def reduce_y(src, land, n, o, piece):
        t = (z + o) % 8
        for j in (1, 3, 2):
            remote(src(4 * t + (y + j) % 4), land.at[o, j - 1], n + o, (s, z * 4 + (y + j) % 4), piece(3)).start()

    def reduce_z(src, land, stage, final, n, o, piece):
        t = (z + o) % 8
        arrived(n + o)
        v = src[4 * t + y].astype(F32) + land[o, 0].astype(F32) + land[o, 1].astype(F32) + land[o, 2].astype(F32)
        if o == 0:
            return v
        stage[o - 1] = v.astype(BF)
        remote(stage.at[o - 1], final.at[o - 1], n + 8, (s, t * 4 + y), piece(7)).start()

    ORDER = (4, 3, 5, 2, 6, 1, 7, 0)

    def spread_half(landing, h):
        for b in range(8):
            cols = pl.ds(pl.multiple_of((8 * h + b) * 128, 128), 128)
            a[:, cols] = landing[h, :, b].reshape(128, 128)

    def nt(x, w):
        return lax.dot_general(x, w, (((1,), (1,)), ((), ())), preferred_element_type=F32)

    at[r] = at0[...]
    gather(at0, lambda k: at.at[k], AG0, lambda k: at.at[pl.ds(0, k)])
    to_rows(lambda d: e.at[d], le.at[r], EA, le.at[pl.ds(0, R - 1)])
    le[r] = e[r]
    for k in range(16):
        block = at[2 * k:2 * k + 2].reshape(128, 128)
        a[:, k * 128:(k + 1) * 128] = block.T
    loads[0].wait()
    loads[1].wait()

    def leaf_update(t, _):
        prod = -nt(a[...], wp0[pl.ds(pl.multiple_of(t * 256, 256), 256), :])
        for b in range(2):
            sb1[:, 2 * t + b] = prod[:, b * 128:(b + 1) * 128].reshape(R, 4, 128).astype(BF)
        return 0

    lax.fori_loop(0, 4, leaf_update, 0)
    to_rows(lambda d: sb1.at[d], lb1.at[pl.ds(1 + r * 8, 8)], A1, lb1.at[pl.ds(0, 8 * (R - 1))])
    lb1[pl.ds(1 + r * 8, 8)] = sb1[r]
    y0[...] = (nt(a[...], qv0[...]) * f0).astype(BF)

    arrived(EA)
    for b in range(8):
        rm[b] = sum(le[4 * b + i, 0].astype(F32) for i in range(4))
    for b in range(4):
        rtq[4 * w4 + b] = sum(le[8 * b + i, 1].astype(F32) for i in range(8)).astype(BF)

    def outer_merge(q, _):
        for i, parts in enumerate(TOP_PIECES):
            v = sum(le[8 * q + d, 2 + k].astype(F32) for d, k in parts).astype(BF)
            gtq[15 * q + i] = v
            zt[17 + 60 * w4 + 15 * q + i] = v
        return 0

    lax.fori_loop(0, 4, outer_merge, 0)
    for p in partners:
        remote(rtq.at[pl.ds(4 * w4, 4)], rtq.at[pl.ds(4 * w4, 4)], RT, (p, r), rtq.at[pl.ds(0, 12)]).start()
        remote(gtq, zt.at[pl.ds(17 + 60 * w4, 60)], ZG, (p, r), zt.at[pl.ds(16, 180)]).start()
    loads[4].wait()
    loads[5].wait()

    def top_given(t, _):
        cols = pl.ds(pl.multiple_of(t * 256, 256), 256)
        xpt[:, cols] = -jnp.dot(g2[...], wp2[:, cols], preferred_element_type=F32)
        return 0

    lax.fori_loop(0, 8, top_given, 0)

    arrived(ZG)

    def mid_pick(j, _):
        v = zt[mt[s // 2, 120 * c + j] + 1]
        gm[j] = v
        zm[17 + 120 * c + j] = v
        return 0

    lax.fori_loop(0, 120, mid_pick, 0, unroll=8)
    for j in range(16, 20):
        gml[j] = gm[j]
    remote(gm.at[pl.ds(0, 120)], zm.at[pl.ds(17 + 120 * c, 120)], ZGM, (p1, r), zm.at[pl.ds(0, 120)]).start()

    arrived(A1)
    table.wait()

    def leaf_merge(q, _):
        lb1[16 * q + 8] = (lb1[16 * q + 8].astype(F32) + lb1[16 * q + 9].astype(F32)).astype(BF)
        return 0

    lax.fori_loop(0, 16, leaf_merge, 0)

    def child_block(core, j):
        b = jnp.where(j < 8, 8 * core, 8 + 120 * core) + j
        return jnp.clip(inv[b // 128, b % 128], 0, 256)

    def for_partner(j, _):
        sp1[j] = lb1[child_block(1 - c, j)]
        return 0

    lax.fori_loop(0, 128, for_partner, 0, unroll=8)
    remote(sp1, rp1, X1, (p1, r), rp1).start()

    def for_own(j, _):
        c1[j] = lb1[child_block(c, j)].astype(F32)
        return 0

    lax.fori_loop(0, 128, for_own, 0, unroll=8)
    arrived(X1)
    c1[...] = c1[...] + rp1[...].astype(F32)

    sba1[...] = (rm[...] + c1[0:8]).astype(BF)
    la1[c, r] = sba1[...]
    gather(sba1, lambda k: la1.at[c, k], G1, lambda k: la1.at[0, pl.ds(0, k)])
    remote(la1.at[c], la1.at[c], D1, (p1, r), la1.at[1 - c]).start()
    to_early_rows(lambda d: gm.at[pl.ds(480 * d // 128, 5)], lg1.at[r], GR1, lg1.at[pl.ds(0, R - 1)])
    lg1[r] = gm[pl.ds(480 * r // 128, 5)]
    spread_half(la1, c)
    arrived(D1)
    spread_half(la1, 1 - c)
    loads[2].wait()
    loads[3].wait()

    for t in range(0, 5, 2):
        prod = nt(a[...], wp1[t * 128:min(t + 2, 5) * 128, :])
        for b in range(t, min(t + 2, 5)):
            sb2[:, b] = prod[:, (b - t) * 128:(b - t + 1) * 128].reshape(R, 4, 128).astype(BF)
    to_rows(lambda d: sb2.at[d], lb2.at[r], A2, lb2.at[pl.ds(0, R - 1)])
    lb2[r] = sb2[r]
    y1[...] = (nt(a[...], qv1[...]) * f1).astype(BF)
    arrived(ZGM)

    def leaf_pick(j, _):
        gl[j] = zm[lt[s, j] + 1]
        return 0

    lax.fori_loop(32, 240, leaf_pick, 0, unroll=8)
    arrived(A2)
    to_early_rows(lambda d: gl.at[pl.ds(960 * d // 128, 8)], lg0.at[r], GR0, lg0.at[pl.ds(0, R - 1)])

    def mid_merge(q, _):
        for i, parts in enumerate(MID_PIECES):
            v = c1[8 + 15 * q + i] - sum(lb2[4 * q + d, k].astype(F32) for d, k in parts)
            vm[1 + 15 * q + i] = v.astype(BF)
        return 0

    lax.fori_loop(0, 8, mid_merge, 0)

    def parent_block(j):
        return jnp.clip(inv[2 + j // 128, j % 128] - 120 * c, 0, 121)

    for j in range(16):
        s3p[j] = vm[parent_block(j)]
    for k, p in enumerate(partners):
        remote(s3p, r3p.at[k], P3, (p, r), r3p).start()
    for k in range(3):
        def top_spread(j, _, k=k):
            s3u[k, j] = vm[parent_block(16 + 60 * (partners[k] % 4) + j)]
            return 0

        lax.fori_loop(0, 60, top_spread, 0, unroll=4)
        remote(s3u.at[k], r3u.at[k], U3, (partners[k], r), r3u).start()
    arrived(RT)
    arrived(P3)
    for j in range(16):
        v = rtq[j].astype(F32) + s3p[j].astype(F32) + sum(r3p[k, j].astype(F32) for k in range(3))
        sba2[j] = v.astype(BF)
    la2[c, r] = sba2[pl.ds(8 * c, 8)]
    gather(sba2.at[pl.ds(8 * c, 8)], lambda k: la2.at[c, k], G2, lambda k: la2.at[0, pl.ds(0, k)])
    arrived(U3)

    def top_sum(j, _):
        v = vm[parent_block(16 + 60 * w4 + j)].astype(F32) + sum(r3u[k, j].astype(F32) for k in range(3))
        ct[j] = v.astype(BF)
        return 0

    lax.fori_loop(0, 60, top_sum, 0, unroll=4)
    remote(la2.at[c], la2.at[c], D2, (p1, r), la2.at[1 - c]).start()
    to_rows(lambda d: ct.at[pl.ds(240 * d // 128, 3)], lc.at[r], CR, lc.at[pl.ds(0, R - 1)])
    lc[r] = ct[pl.ds(240 * r // 128, 3)]
    spread_half(la2, c)
    arrived(D2)
    spread_half(la2, 1 - c)
    y2[...] = (nt(a[...], qv2[...]) * f2).astype(BF)

    def top_partial(t, _):
        cols = pl.ds(pl.multiple_of(t * 256, 256), 256)
        v = xpt[:, cols] + jnp.dot(y2[...], qv2[:, cols], preferred_element_type=F32)
        for b in range(2):
            sbx[t // 4, :, 2 * (t % 4) + b] = v[:, b * 128:(b + 1) * 128].reshape(R, 4, 128).astype(BF)
        return 0

    lax.fori_loop(0, 8, top_partial, 0)
    remote(sbx.at[1 - c], rbx, HX2, (p1, r), rbx).start()
    prod = nt(a[...], wp2[...])
    arrived(CR)
    for b in range(3):
        v = lc[:, b].astype(F32).reshape(128, 128) - prod[:, b * 128:(b + 1) * 128]
        tmp[b * 128:(b + 1) * 128] = v.T
    o_con[...] = jnp.where(row240 < upd2 - 240 * m2, tmp[pl.ds(off2, 240), :], 0.0).astype(BF)
    arrived(HX2)

    def reduce_half(mine, other, both, land, stage, final, n):
        for o in ORDER:
            t = (z + o) % 8
            rows4 = pl.ds(4 * t, 4)
            both[rows4] = (mine[c, rows4].astype(F32) + other[rows4].astype(F32)).astype(BF)
            reduce_y(lambda d: both.at[d], land, n, o, lambda k: land.at[0, pl.ds(0, k)])
        for o in ORDER:
            v = reduce_z(both, land, stage, final, n, o, lambda k: final.at[pl.ds(0, k)])
        arrived(n + 8)
        for o in range(7):
            v = v + final[o].astype(F32)
        return v

    xs2[...] = reduce_half(sbx, rbx, sby, ry, sz, lz, RS2)
    remote(xs2, xx2, XX2, (p2, r), xx2).start()
    arrived(XX2)
    for b in range(8):
        zt[1 + 8 * c + b] = ((xs2[b] + xx2[b]) * live(piv2, 8 * c + b)).astype(BF)
    remote(zt.at[pl.ds(1 + 8 * c, 8)], zt.at[pl.ds(1 + 8 * c, 8)], ZX2, (p1, r), zt.at[pl.ds(0, 8)]).start()
    arrived(ZX2)

    for j in range(16):
        v = zt[mt[s // 2, 120 * c + j] + 1]
        gml[j] = v
        zm[17 + 120 * c + j] = v
    to_late_rows(lambda d: gml.at[pl.ds(480 * d // 128, 5)], lg1.at[r], GR1, lg1.at[pl.ds(0, R - 1)])

    @pl.when(r < LATE)
    def _():
        lg1[r] = gml[pl.ds(480 * jnp.minimum(r, LATE - 1) // 128, 5)]

    remote(gml.at[pl.ds(0, 16)], zm.at[pl.ds(17 + 120 * c, 16)], ZGL, (p1, r), zm.at[pl.ds(0, 16)]).start()
    to_rows(lambda d: zt.at[1 + 4 * w4 + d // 8], lot.at[r], OT, lot.at[pl.ds(0, R - 1)])
    lot[r] = zt[1 + 4 * w4 + r // 8]
    arrived(GR1)
    for b in range(5):
        g1[:, b * 128:(b + 1) * 128] = lg1[:, b].reshape(128, 128)

    def mid_partial(i, _):
        t = (4 * (1 - c) + i) % 8
        cols = pl.ds(pl.multiple_of(t * 256, 256), 256)
        v = jnp.dot(y1[...], qv1[:, cols], preferred_element_type=F32) - jnp.dot(
            g1[...], wp1[:, cols], preferred_element_type=F32
        )
        for b in range(2):
            sbx1[t // 4, :, 2 * (t % 4) + b] = v[:, b * 128:(b + 1) * 128].reshape(R, 4, 128).astype(BF)
        return 0

    lax.fori_loop(0, 4, mid_partial, 0)
    remote(sbx1.at[1 - c], rbx1, HX1, (p1, r), rbx1).start()
    lax.fori_loop(4, 8, mid_partial, 0)
    arrived(HX1)
    xsum = reduce_half(sbx1, rbx1, sby1, ry1, sz1, lz1, RS1)
    for b in range(8):
        v = (xsum[b] * live(piv1, 8 * c + b)).astype(BF)
        xsb1[b] = v
        zm[1 + 8 * c + b] = v
    remote(xsb1, zm.at[pl.ds(1 + 8 * c, 8)], ZX1, (p1, r), zm.at[pl.ds(0, 8)]).start()
    arrived(ZX1)
    arrived(ZGL)

    lax.fori_loop(0, 32, leaf_pick, 0, unroll=8)
    to_late_rows(lambda d: gl.at[pl.ds(960 * d // 128, 8)], lg0.at[r], GR0, lg0.at[pl.ds(0, R - 1)])
    lg0[r] = gl[pl.ds(960 * r // 128, 8)]
    to_rows(lambda d: xsb1.at[d // 4], lom.at[r], OM, lom.at[pl.ds(0, R - 1)])
    lom[r] = xsb1[r // 4]
    arrived(OT)
    tmp[0:128] = lot[...].astype(F32).reshape(128, 128).T
    o_top[...] = tmp[pl.ds(pl.multiple_of(16 * (r % 8), 16), 16), :].astype(BF)
    arrived(GR0)
    for b in range(8):
        g0[:, b * 128:(b + 1) * 128] = lg0[:, b].reshape(128, 128)

    def leaf_tile(o):
        t = (z + o) % 8
        cols = pl.ds(pl.multiple_of(t * 256, 256), 256)
        v = jnp.dot(y0[...], qv0[:, cols], preferred_element_type=F32) - jnp.dot(
            g0[...], wp0[:, cols], preferred_element_type=F32
        )
        sbl[pl.ds(4 * t, 4)] = v.T.astype(BF).reshape(4, 64, 128)
        reduce_y(lambda d: sbl.at[d], ryl, RS0, o, lambda k: ryl.at[0, pl.ds(0, k)])

    def leaf_sum(o):
        return reduce_z(sbl, ryl, szl, lzl, RS0, o, lambda k: lzl.at[pl.ds(0, k)])

    for k in range(8):
        leaf_tile(ORDER[k])
        if k >= 4:
            leaf_sum(ORDER[k - 4])
    for k in range(4, 8):
        xl = leaf_sum(ORDER[k])
    arrived(OM)
    tmp[0:128] = lom[...].astype(F32).reshape(128, 128).T
    o_mid[...] = tmp[pl.ds(pl.multiple_of(32 * (r % 4), 32), 32), :].astype(BF)
    arrived(RS0 + 8)
    for o in range(7):
        xl = xl + lzl[o].astype(F32)
    o_leaf[...] = (xl * f0).astype(BF)

    for n in landed:
        sent(n)


SCRATCH = [
    ((1024, 2048), BF), ((640, 2048), BF), ((384, 2048), BF), ((64, 2048), BF), ((32, 2048), BF), ((16, 2048), BF),
    ((64, 128), BF), ((R, 5, 4, 128), BF),
    ((R, 64, 128), BF), ((128, 2048), BF), ((128, 64), BF), ((128, 32), BF), ((128, 16), BF), ((R, 5, 4, 128), BF),
    ((R, 8, 4, 128), BF), ((264, 4, 128), BF), ((128, 4, 128), BF), ((128, 4, 128), BF), ((128, 4, 128), F32),
    ((8, 4, 128), F32), ((8, 4, 128), BF), ((2, R, 8, 4, 128), BF), ((R, 5, 4, 128), BF), ((R, 5, 4, 128), BF),
    ((122, 4, 128), BF),
    ((16, 4, 128), BF), ((3, 16, 4, 128), BF), ((3, 60, 4, 128), BF), ((3, 60, 4, 128), BF), ((16, 4, 128), BF),
    ((16, 4, 128), BF), ((2, R, 8, 4, 128), BF), ((60, 4, 128), BF), ((257, 4, 128), BF), ((61, 4, 128), BF),
    ((R, 3, 4, 128), BF), ((128, 384), BF), ((128, 2048), F32), ((2, R, 8, 4, 128), BF), ((R, 8, 4, 128), BF),
    ((R, 8, 4, 128), BF), ((8, 3, 8, 4, 128), BF), ((7, 8, 4, 128), BF), ((7, 8, 4, 128), BF), ((8, 4, 128), F32), ((8, 4, 128), F32), ((121, 4, 128), BF), ((20, 4, 128), BF),
    ((257, 4, 128), BF), ((R, 5, 4, 128), BF), ((128, 640), BF),
    ((2, R, 8, 4, 128), BF), ((R, 8, 4, 128), BF), ((R, 8, 4, 128), BF), ((8, 3, 8, 4, 128), BF), ((7, 8, 4, 128), BF), ((7, 8, 4, 128), BF), ((8, 4, 128), BF),
    ((240, 4, 128), BF), ((R, 8, 4, 128), BF), ((128, 1024), BF), ((R, 64, 128), BF), ((8, 3, 64, 128), BF),
    ((7, 64, 128), BF), ((7, 64, 128), BF),
    ((R, 4, 128), BF), ((R, 4, 128), BF),
]


def hand_over(*refs):
    for k in range(4):
        refs[4 + k][...] = refs[k][...]


def body(
    leaf_inverse, leaf_panel, mid_inverse, mid_panel, top_inverse, top_panel,
    leaf_rhs, mid_rhs, top_rhs, outer_solution, leaf_targets, mid_targets, front_counts,
):
    vmem = pl.BlockSpec(memory_space=pltpu.VMEM)
    smem = pl.BlockSpec(memory_space=pltpu.SMEM)
    hbm = pl.BlockSpec(memory_space=pl.ANY)
    outs = pl.pallas_call(
        kernel,
        out_shape=tuple(jax.ShapeDtypeStruct((n, 128), BF) for n in (64, 32, 16, 240)),
        in_specs=[vmem] * 4 + [hbm] * 6 + [vmem] * 2 + [smem] * 3,
        out_specs=(vmem,) * 4,
        scratch_shapes=[pltpu.VMEM(shape, kind) for shape, kind in SCRATCH]
        + [pltpu.VMEM((384, 128), F32), pltpu.VMEM((8, 128), jnp.int32), pltpu.SMEM((8, 128), jnp.int32)]
        + [pltpu.SemaphoreType.DMA, pltpu.SemaphoreType.DMA((6,)), pltpu.SemaphoreType.DMA((NSEM,)), pltpu.SemaphoreType.DMA((NSEM,))],
        compiler_params=pltpu.CompilerParams(
            collective_id=0, has_side_effects=True, vmem_limit_bytes=56 * 1024 * 1024
        ),
        name="solve",
    )(
        leaf_rhs.T, mid_rhs.T, top_rhs.T, outer_solution.T,
        leaf_panel, leaf_inverse, mid_panel, mid_inverse, top_panel, top_inverse,
        leaf_targets, mid_targets, leaf_targets, mid_targets, front_counts.T,
    )
    shapes = tuple(jax.ShapeDtypeStruct(out.shape, BF) for out in outs)
    outs = pl.pallas_call(hand_over, out_shape=shapes, in_specs=[vmem] * 4, out_specs=(vmem,) * 4, name="hand_over")(*outs)
    return tuple(out.T for out in outs)


def solution(mesh):
    stacked = P(("leaf", "rows"), None)
    side = P(None, ("leaf", "rows"))
    return jax.shard_map(
        body,
        mesh=mesh,
        in_specs=(stacked,) * 6 + (side,) * 4 + (P(),) * 3,
        out_specs=(side,) * 4,
        check_vma=False,
    )
```
